32 devices in a mesh: alt: 2 (over x), strip: 16 (over z, y, core).
Axes of the slice: x: 2, y: 2, z: 4, core: 2. Of those that a mesh axis runs over, the one named last changes fastest.
Arguments:
- screens: bfloat16 [4, 512, 512], P('alt', 'strip'), may hold values from -2.390625 to 2.390625
- row_offset: int32 [2, 4, 2], replicated, may hold values from 0 to 341, as said below
- col_offset: int32 [2, 4, 2], replicated, may hold values from 0 to 341, as said below
- layer_bin: int32 [4], replicated, may hold values from 0 to 15
- illumination: float32 [16, 12800], P(None, ('alt', 'strip')), may hold values from 0.3 to 1
- reconstructor: bfloat16 [2, 12800, 6000], P(None, ('alt', 'strip')), may hold values from -0.0390625 to 0.0390625
- sat_code: int32 [6000], replicated, may hold values from 1 to 16
Outputs:
- slopes: float32 [2, 2, 12800], P(None, None, ('alt', 'strip'))
- commands: float32 [2, 6000], replicated
The draws below stay inside these ranges and needn't reach their ends.
Inputs may be any that keep to these rules, and one draw needn't show every extreme that they name: Every footprint lies inside the screen: row_offset[f, l, g] + (319) shrink_l <= 511. Every footprint lies inside the screen: col_offset[f, l, g] + (319) shrink_l <= 511.
All inputs are finite; a program needn't handle non-finite values.
Results may differ from the reference program's by a relative error of at most 0.0028.
Values sent between devices are 32-bit elements; how exact they have to be, the bound alone decides.
A program may use at most 64 MiB of HBM per device.

```python
import math
import jax
import jax.numpy as jnp
from jax import lax

LENSLETS = 80
PIXELS = 4
GUIDE_STARS = 2
FRAMES = 2
ACTUATORS = 6000
SCREEN_ROWS = 512
COLUMNS = 512
LAYERS = 4
PUPIL_PIX = 320
WINDOW = 384
SUBAPS_ALL = 12800


def geometry(key):
    base = jax.random.fold_in(key, 7013)
    keys = jax.random.split(base, 6)
    bins = jax.random.randint(keys[0], (LAYERS,), 0, 16, dtype=jnp.int32)
    order = jax.random.permutation(keys[1], LAYERS)
    bins = bins.at[order[0]].set(0).at[order[1]].set(15)
    stars = jnp.arange(GUIDE_STARS, dtype=jnp.int32)
    pattern = (2 * stars - (GUIDE_STARS - 1)) * 3 // (GUIDE_STARS - 1)
    dir_rows = jax.random.permutation(keys[2], pattern)
    dir_cols = jax.random.permutation(keys[3], pattern)
    wind_reach_rows = max(1, (SCREEN_ROWS - PUPIL_PIX) // 48)
    wind_reach_cols = max(1, (COLUMNS - PUPIL_PIX) // 48)
    wind_rows = jax.random.randint(keys[4], (LAYERS,), -wind_reach_rows, wind_reach_rows + 1, dtype=jnp.int32)
    wind_cols = jax.random.randint(keys[5], (LAYERS,), -wind_reach_cols, wind_reach_cols + 1, dtype=jnp.int32)
    return (bins, dir_rows, dir_cols, wind_rows, wind_cols)


def placement(bins, directions, winds, extent):
    half_span = (PUPIL_PIX - 1) * (32 - bins) // 64
    full_span = ((PUPIL_PIX - 1) * (32 - bins) + 31) // 32
    displaced = directions[None, :] * bins[:, None] * (extent - PUPIL_PIX) // 32
    first = extent // 2 - half_span[:, None] + displaced
    frame_steps = jnp.arange(FRAMES, dtype=jnp.int32)
    starts = first[None, :, :] + frame_steps[:, None, None] * winds[None, :, None]
    upper = extent - 1 - full_span
    return jnp.clip(starts, 0, upper[None, :, None]).astype(jnp.int32)


def draw_layer_bin(key, part):
    bins, dir_rows, dir_cols, wind_rows, wind_cols = geometry(key)
    return bins.astype(jnp.int32)


def draw_row_offset(key, part):
    bins, dir_rows, dir_cols, wind_rows, wind_cols = geometry(key)
    return placement(bins, dir_rows, wind_rows, SCREEN_ROWS)


def draw_col_offset(key, part):
    bins, dir_rows, dir_cols, wind_rows, wind_cols = geometry(key)
    return placement(bins, dir_cols, wind_cols, COLUMNS)


def place_ends(result, key, low, top_value):
    place = [jax.random.randint(jax.random.fold_in(key, axis), (), 0, length) for axis, length in enumerate(result.shape)]
    longest = result.shape.index(max(result.shape))
    next_to = place[:longest] + [(place[longest] + 1) % result.shape[longest]] + place[longest + 1:]
    return result.at[tuple(place)].set(low).at[tuple(next_to)].set(top_value)


def block_levels(stream_key, shape, cuts, smallest, high):
    factor_of = 1.0
    for dim, shards_of in cuts:
        steps = jax.random.uniform(jax.random.fold_in(jax.random.fold_in(stream_key, 6), dim), (shards_of,), jnp.float32, smallest / len(cuts), high / len(cuts))
        factor_of = factor_of * jnp.repeat(jnp.exp(steps), shape[dim] // shards_of).reshape((-1,) + (1,) * (len(shape) - 1 - dim))
    return factor_of


def noise(rng, dims, deviation, reach, cuts=(), kind=jnp.bfloat16):
    entries = jax.random.normal(rng, dims, jnp.float32) * deviation
    if len(cuts) > 0:
        entries = block_levels(rng, dims, cuts, -0.22, 0.18) * entries
    return jnp.clip(entries, min=-reach, max=reach).astype(kind)


def setup_inputs(seed: int = 0) -> dict:
    arg_keys = jax.random.split(jax.random.key(seed), 8)
    screens = noise(arg_keys[0], (LAYERS, SCREEN_ROWS, COLUMNS), 0.3, 2.390625, ((0, 2), (1, 16)))
    row_offset = draw_row_offset(jax.random.fold_in(arg_keys[7], 71), 0)
    col_offset = draw_col_offset(jax.random.fold_in(arg_keys[7], 71), 0)
    layer_bin = draw_layer_bin(jax.random.fold_in(arg_keys[7], 71), 0)
    illumination = jnp.clip(jnp.exp(math.log(1.0) - 1.2039728 * jax.random.uniform(arg_keys[4], (PIXELS * PIXELS, SUBAPS_ALL), jnp.float32) ** block_levels(arg_keys[4], (PIXELS * PIXELS, SUBAPS_ALL), ((1, 32),), -0.2, 0.2)), 0.3, 1.0)
    reconstructor = noise(arg_keys[5], (2, SUBAPS_ALL, ACTUATORS), (2 * SUBAPS_ALL) ** -0.5, 0.0390625, ((1, 32),))
    sat_code = place_ends(jax.random.randint(arg_keys[6], (ACTUATORS,), 1, 17), jax.random.fold_in(arg_keys[6], 1), 1, 16).astype(jnp.int32)
    return dict(screens=screens, row_offset=row_offset, col_offset=col_offset, layer_bin=layer_bin, illumination=illumination, reconstructor=reconstructor, sat_code=sat_code)


highest = lax.Precision.HIGHEST
loop_gain = 0.5
code_step = 0.125
bin_step = 0.03125


def bilinear(offsets):
    return jnp.maximum(0.0, 1.0 - jnp.abs(offsets))


def dft_tables():
    padded = 2 * PIXELS
    freq_index = jnp.arange(padded * padded, dtype=jnp.int32)
    freq_row = freq_index // padded
    freq_col = freq_index % padded
    pix_index = jnp.arange(PIXELS * PIXELS, dtype=jnp.int32)
    pix_row = pix_index // PIXELS
    pix_col = pix_index % PIXELS
    turn_count = (freq_row[:, None] * pix_row[None, :] + freq_col[:, None] * pix_col[None, :]) % padded
    angles = turn_count.astype(jnp.float32) * (2.0 * math.pi / padded)
    coord_row = ((freq_row + PIXELS) % padded - PIXELS).astype(jnp.float32)
    coord_col = ((freq_col + PIXELS) % padded - PIXELS).astype(jnp.float32)
    return jnp.cos(angles), jnp.sin(angles), coord_row, coord_col


def centroids(pupil_phase, illumination, tables):
    cosine, sine_table, coord_row, coord_col = tables
    field_re = illumination * jnp.cos(pupil_phase)
    field_im = illumination * jnp.sin(pupil_phase)
    real_part = jnp.dot(cosine, field_re, precision=highest) + jnp.dot(sine_table, field_im, precision=highest)
    imag_part = jnp.dot(cosine, field_im, precision=highest) - jnp.dot(sine_table, field_re, precision=highest)
    intensity = real_part * real_part + imag_part * imag_part
    flux_sum = jnp.sum(intensity, axis=0)
    slope_row = jnp.sum(intensity * coord_row[:, None], axis=0) / flux_sum
    slope_col = jnp.sum(intensity * coord_col[:, None], axis=0) / flux_sum
    return jnp.stack([slope_row, slope_col])


def project_frame(screens, row_start, col_start, shrinks):
    pupil_idx = jnp.arange(PUPIL_PIX, dtype=jnp.float32)
    window_idx = jnp.arange(WINDOW, dtype=jnp.float32)

    def one_layer(running, inputs):
        screen, tops, lefts, shrink = inputs
        widened = jnp.pad(screen, ((0, WINDOW), (0, WINDOW)))
        weights = bilinear(window_idx[None, :] - pupil_idx[:, None] * shrink)

        def one_star(top_row, left_col):
            window_block = lax.dynamic_slice(widened, (top_row, left_col), (WINDOW, WINDOW)).astype(jnp.float32)
            across = jnp.dot(window_block, weights.T, precision=highest)
            return jnp.dot(weights, across, precision=highest)

        return running + jax.vmap(one_star)(tops, lefts), None

    initial = jnp.zeros((GUIDE_STARS, PUPIL_PIX, PUPIL_PIX), jnp.float32)
    summed, unused = lax.scan(one_layer, initial, (screens, row_start, col_start, shrinks))
    return summed


def reference(screens, row_offset, col_offset, layer_bin, illumination, reconstructor, sat_code):
    shrinks = 1.0 - layer_bin.astype(jnp.float32) * bin_step
    tables = dft_tables()
    slope_list = []
    for frame_no in range(FRAMES):
        summed = project_frame(screens, row_offset[frame_no], col_offset[frame_no], shrinks)
        pupil_phase = summed.reshape(GUIDE_STARS, LENSLETS, PIXELS, LENSLETS, PIXELS)
        pupil_phase = pupil_phase.transpose(2, 4, 0, 1, 3).reshape(PIXELS * PIXELS, SUBAPS_ALL)
        slope_list.append(centroids(pupil_phase, illumination, tables))
    slopes = jnp.stack(slope_list)
    rounded = slopes.astype(jnp.bfloat16).reshape(FRAMES, 2 * SUBAPS_ALL)
    updates = jnp.dot(rounded, reconstructor.reshape(2 * SUBAPS_ALL, ACTUATORS), preferred_element_type=jnp.float32)
    limits = sat_code.astype(jnp.float32) * code_step
    first_cmd = jnp.clip(loop_gain * updates[0], -limits, limits)
    second_cmd = jnp.clip(first_cmd + loop_gain * updates[1], -limits, limits)
    return slopes, jnp.stack([first_cmd, second_cmd])
```

```python
import functools
import math

import jax
import jax.numpy as jnp
from jax import lax
from jax.experimental import pallas as pl
from jax.experimental.pallas import tpu as pltpu
from jax.sharding import PartitionSpec as P

LENSLETS = 80
PIXELS = 4
GUIDE_STARS = 2
FRAMES = 2
ACTUATORS = 6000
PUPIL_PIX = 320
WINDOW = 384
SUBAPS_ALL = 12800


highest = lax.Precision.HIGHEST
loop_gain = 0.5
code_step = 0.125
bin_step = 0.03125


def bilinear(offsets):
    return jnp.maximum(0.0, 1.0 - jnp.abs(offsets))


def dft_tables():
    padded = 2 * PIXELS
    freq_index = jnp.arange(padded * padded, dtype=jnp.int32)
    freq_row = freq_index // padded
    freq_col = freq_index % padded
    pix_index = jnp.arange(PIXELS * PIXELS, dtype=jnp.int32)
    pix_row = pix_index // PIXELS
    pix_col = pix_index % PIXELS
    turn_count = (
        freq_row[:, None] * pix_row[None, :] + freq_col[:, None] * pix_col[None, :]
    ) % padded
    angles = turn_count.astype(jnp.float32) * (2.0 * math.pi / padded)
    coord_row = ((freq_row + PIXELS) % padded - PIXELS).astype(jnp.float32)
    coord_col = ((freq_col + PIXELS) % padded - PIXELS).astype(jnp.float32)
    return (jnp.cos(angles), jnp.sin(angles), coord_row, coord_col)


def centroids(pupil_phase, illumination, tables):
    cosine, sine_table, coord_row, coord_col = tables
    field_re = illumination * jnp.cos(pupil_phase)
    field_im = illumination * jnp.sin(pupil_phase)
    real_part = jnp.dot(cosine, field_re, precision=highest) + jnp.dot(
        sine_table, field_im, precision=highest
    )
    imag_part = jnp.dot(cosine, field_im, precision=highest) - jnp.dot(
        sine_table, field_re, precision=highest
    )
    intensity = real_part * real_part + imag_part * imag_part
    flux_sum = jnp.sum(intensity, axis=0)
    slope_row = jnp.sum(intensity * coord_row[:, None], axis=0) / flux_sum
    slope_col = jnp.sum(intensity * coord_col[:, None], axis=0) / flux_sum
    return jnp.stack([slope_row, slope_col])


def shards(screens, row_offset, col_offset, layer_bin, illumination, reconstructor, sat_code):
    layer_dev = screens.shape[0]
    rows_here = screens.shape[1]
    count_here = illumination.shape[1]
    group_pos = lax.axis_index("alt")
    strip_pos = lax.axis_index("strip")
    row_global = strip_pos * rows_here + jnp.arange(rows_here, dtype=jnp.int32)
    pupil_idx = jnp.arange(PUPIL_PIX, dtype=jnp.float32)
    window_idx = jnp.arange(WINDOW, dtype=jnp.float32)
    widened_layers = [
        jnp.pad(screens[layer_no], ((0, 0), (0, WINDOW))) for layer_no in range(layer_dev)
    ]
    frame_terms = []
    for frame_no in range(FRAMES):
        running = jnp.zeros((PIXELS, PIXELS, GUIDE_STARS, LENSLETS, LENSLETS), jnp.float32)
        for layer_no in range(layer_dev):
            layer_pos = group_pos * layer_dev + layer_no
            tops = lax.dynamic_index_in_dim(row_offset[frame_no], layer_pos, 0, keepdims=False)
            lefts = lax.dynamic_index_in_dim(col_offset[frame_no], layer_pos, 0, keepdims=False)
            bin_value = lax.dynamic_index_in_dim(layer_bin, layer_pos, 0, keepdims=False)
            shrink = 1.0 - bin_value.astype(jnp.float32) * bin_step
            col_weights = bilinear(window_idx[None, :] - pupil_idx[:, None] * shrink)
            widened = widened_layers[layer_no]

            def cut_columns(left_col):
                return lax.dynamic_slice_in_dim(widened, left_col, WINDOW, 1)

            strips = jax.vmap(cut_columns)(lefts).astype(jnp.float32)
            across = jnp.einsum("drc,jc->drj", strips, col_weights, precision=highest)
            offsets = (row_global[None, :] - tops[:, None]).astype(jnp.float32)
            row_weights = bilinear(offsets[:, None, :] - pupil_idx[None, :, None] * shrink)
            running = running + jnp.einsum(
                "dapr,drbq->pqdab",
                row_weights.reshape(GUIDE_STARS, LENSLETS, PIXELS, rows_here),
                across.reshape(GUIDE_STARS, rows_here, LENSLETS, PIXELS),
                precision=highest,
            )
        frame_terms.append(running.reshape(PIXELS * PIXELS, SUBAPS_ALL))
    phase_terms = jnp.concatenate(frame_terms, axis=0)
    partly = lax.psum_scatter(phase_terms, "alt", scatter_dimension=1, tiled=True)
    owned = lax.psum_scatter(partly, "strip", scatter_dimension=1, tiled=True)
    pupil_phase = owned.reshape(FRAMES, PIXELS * PIXELS, count_here)
    tables = dft_tables()
    slopes = jnp.stack(
        [centroids(pupil_phase[frame_no], illumination, tables) for frame_no in range(FRAMES)]
    )
    rounded = slopes.astype(jnp.bfloat16).reshape(FRAMES, 2 * count_here)
    partial_value = jnp.dot(
        rounded,
        reconstructor.reshape(2 * count_here, ACTUATORS),
        preferred_element_type=jnp.float32,
    )
    updates = lax.psum(partial_value, ("alt", "strip"))
    limits = sat_code.astype(jnp.float32) * code_step
    first_cmd = jnp.clip(loop_gain * updates[0], -limits, limits)
    second_cmd = jnp.clip(first_cmd + loop_gain * updates[1], -limits, limits)
    return (slopes, jnp.stack([first_cmd, second_cmd]))


MESH = pl.DeviceIdType.MESH


def pair_gain(distance):
    turn = 2.0 * math.pi / (2 * PIXELS)
    return 4.0 * sum(k * math.sin(turn * k * distance) for k in range(1, PIXELS))


SPLIT = 2


def padded_rows(arcs):
    return -(-arcs * FRAMES * PIXELS // 16) * 16


def packed_rows(arcs):
    full = PUPIL_PIX // 128
    return FRAMES * PIXELS * (full * arcs + (arcs + 1) // 2)


def fused_kernel(
    depth,
    block,
    scr_hbm,
    row_hbm,
    col_hbm,
    bin_hbm,
    ill_hbm,
    rec_hbm,
    sat_hbm,
    slopes_out,
    upd_out,
    scr_ref,
    row_ref,
    col_ref,
    bin_ref,
    ill_ref,
    scr_all,
    colw,
    roww,
    rhs,
    acc,
    ysend,
    yown,
    yrecv,
    zsend,
    zrecv,
    phiq,
    illq,
    slope_sc,
    rec,
    upd,
    part,
    zsum,
    sat_raw,
    sat,
    in_sem,
    rec_sem,
    x_send,
    x_recv,
    core_send,
    core_recv,
    fwd_send,
    fwd_recv,
    y_send,
    y_recv,
    z_send,
    z_recv,
    a_send,
    a_recv,
    b_send,
    b_recv,
    sat_sem,
    c_send,
    c_recv,
):
    layer_dev, rows_here, columns = scr_ref.shape
    count_here = ill_ref.shape[1]
    arcs = count_here // LENSLETS
    chunk_rows = padded_rows(arcs)
    full = PUPIL_PIX // 128
    rest = PUPIL_PIX - full * 128
    rows_chip = 2 * rows_here
    actuators = rec_hbm.shape[2]

    loads = [
        pltpu.make_async_copy(src, dst, in_sem.at[n])
        for n, (src, dst) in enumerate(
            (
                (scr_hbm, scr_ref),
                (row_hbm, row_ref),
                (col_hbm, col_ref),
                (bin_hbm, bin_ref),
                (ill_hbm, ill_ref),
            )
        )
    ]
    for load in loads:
        load.start()
    rec_copy = pltpu.make_async_copy(rec_hbm, rec, rec_sem)
    rec_copy.start()
    sat_load = pltpu.make_async_copy(sat_hbm, sat_raw, sat_sem)
    sat_load.start()

    x = lax.axis_index("alt")
    strip = lax.axis_index("strip")
    core = strip % 2
    y = (strip // 2) % 2
    z = strip // 4
    me = (x * 2 + y) * 2 + core

    offsets = ((1, 1, 0), (1, 1, 1), (1, 0, 0), (1, 0, 1), (0, 1, 0), (0, 1, 1), (0, 0, 1))

    def place(n):
        dx, dy, dc = offsets[n]
        return ((x + dx) % 2, (y + dy) % 2, (core + dc) % 2)

    def plane(n):
        px, py, pc = place(n)
        return (px, (z * 2 + py) * 2 + pc)

    def slot(n):
        px, py, pc = place(n)
        return (px * 2 + py) * 2 + pc

    def depth_dev(zpos):
        return (x, (zpos * 2 + y) * 2 + core)

    barrier = pltpu.get_barrier_semaphore()
    for n in range(7):
        pl.semaphore_signal(barrier, inc=1, device_id=plane(n), device_id_type=MESH)
    for k in range(1, depth):
        pl.semaphore_signal(barrier, inc=1, device_id=depth_dev((z + k) % depth), device_id_type=MESH)

    own = pl.ds(x * layer_dev, layer_dev)
    loads[0].wait()
    for li in range(layer_dev):
        scr_all[core, x * layer_dev + li] = scr_ref[li].astype(jnp.float32)
    pl.semaphore_wait(barrier, 7 + depth - 1)

    def remote(src, dst, send, recv, device):
        copy = pltpu.make_async_remote_copy(
            src_ref=src, dst_ref=dst, send_sem=send, recv_sem=recv, device_id=device, device_id_type=MESH
        )
        copy.start()
        return copy

    own_block = scr_all.at[core, own]
    x_copies = []
    for li in range(layer_dev):
        piece = scr_all.at[core, x * layer_dev + li]
        x_copies.append(remote(piece, piece, x_send.at[li], x_recv.at[li], (1 - x, strip)))
    core_dev = (x, (z * 2 + y) * 2 + 1 - core)
    core_copy = remote(own_block, own_block, core_send, core_recv, core_dev)

    for load in loads[1:]:
        load.wait()
    col_pos = lax.broadcasted_iota(jnp.int32, (columns, PUPIL_PIX), 0).astype(jnp.float32)
    lane = lax.broadcasted_iota(jnp.int32, (1, PUPIL_PIX), 1)
    q_of = (
        (lane >= LENSLETS).astype(jnp.int32)
        + (lane >= 2 * LENSLETS).astype(jnp.int32)
        + (lane >= 3 * LENSLETS).astype(jnp.int32)
    )
    pupil_col = ((lane - q_of * LENSLETS) * PIXELS + q_of).astype(jnp.float32)
    row_lane = lax.broadcasted_iota(jnp.int32, (chunk_rows, 2 * rows_chip), 1)
    row_pos = (row_lane % rows_chip + (z * 2 + y) * rows_chip).astype(jnp.float32)
    row_sub = lax.broadcasted_iota(jnp.int32, (chunk_rows, 2 * rows_chip), 0)
    row_base = (row_sub // 8) * PIXELS + row_sub % PIXELS
    row_frame = (row_sub // PIXELS) % FRAMES
    seg = 2 * rows_chip
    groups = [(rel, li) for rel in range(2) for li in range(layer_dev)]

    for rel, li in groups:
        layer = ((x + rel) % 2) * layer_dev + li
        shrink = 1.0 - bin_ref[layer].astype(jnp.float32) * bin_step
        reach = pupil_col * shrink
        for f in range(FRAMES):
            left = col_ref[f, x, layer].astype(jnp.float32)
            weight = bilinear(col_pos - (reach + left))
            colw[f, rel * layer_dev + li] = weight.astype(jnp.bfloat16)

    tops = [
        [row_ref[f, x, ((x + rel) % 2) * layer_dev + li].astype(jnp.float32) for rel, li in groups]
        for f in range(FRAMES)
    ]
    shrinks = [
        1.0 - bin_ref[((x + rel) % 2) * layer_dev + li].astype(jnp.float32) * bin_step for rel, li in groups
    ]
    for zpos in range(depth):
        for ypos in range(2):
            first = ((zpos * 2 + ypos) * 2 + core) * (arcs * PIXELS)
            pupil_row = (row_base + first).astype(jnp.float32)
            for f in range(FRAMES):
                for n in range(len(groups)):
                    weight = bilinear(row_pos - tops[f][n] - pupil_row * shrinks[n])
                    weight = jnp.where(row_frame == f, weight, 0.0)
                    at = (n * FRAMES + f) * seg
                    roww[ypos, zpos * chunk_rows : (zpos + 1) * chunk_rows, at : at + seg] = weight.astype(
                        jnp.bfloat16
                    )
    for p in range(PIXELS):
        for q in range(PIXELS):
            for f in range(FRAMES):
                illq[q, f * PIXELS + p : f * PIXELS + p + 1, :] = ill_ref[p * PIXELS + q : p * PIXELS + q + 1, :]

    sat_load.wait()
    for n in range(8):
        width = min(block, actuators - n * block)
        sat[n, 0, :width] = sat_raw[n * block : n * block + width]

    def across(rel, layers):
        for li in layers:
            layer = ((x + rel) % 2) * layer_dev + li
            rows = scr_all[:, layer].reshape(rows_chip, columns).astype(jnp.bfloat16)
            for f in range(FRAMES):
                value = jnp.dot(rows, colw[f, rel * layer_dev + li], preferred_element_type=jnp.float32)
                high = value.astype(jnp.bfloat16)
                low = (value - high.astype(jnp.float32)).astype(jnp.bfloat16)
                at = ((rel * layer_dev + li) * FRAMES + f) * seg
                rhs[at : at + rows_chip, :] = high
                rhs[at + rows_chip : at + seg, :] = low

    core_copy.wait()
    def project(ypos, lo, hi):
        value = jnp.dot(roww[ypos, :, lo:hi], rhs[lo:hi, :], preferred_element_type=jnp.float32)
        return value.reshape(depth, chunk_rows, PUPIL_PIX)

    step = FRAMES * seg
    across(0, range(layer_dev))
    fwd_copies = []
    for li in range(layer_dev):
        if li == 1:
            for ypos in range(2):
                acc[ypos] = project(ypos, 0, layer_dev * step)
        x_copies[li].wait_recv()
        piece = scr_all.at[core, (1 - x) * layer_dev + li]
        fwd_copies.append(remote(piece, piece, fwd_send.at[li], fwd_recv.at[li], core_dev))
    for li in range(layer_dev):
        fwd_copies[li].wait()
        across(1, [li])
        if li < layer_dev - 1:
            for ypos in range(2):
                acc[ypos] += project(ypos, (layer_dev + li) * step, (layer_dev + li + 1) * step)
    last = (2 * layer_dev - 1) * step

    def finish(ypos, zpos, out):
        rows = pl.ds(pl.multiple_of(zpos * chunk_rows, chunk_rows), chunk_rows)
        value = jnp.dot(roww[ypos, rows, last:], rhs[last:, :], preferred_element_type=jnp.float32)
        value = value + acc[ypos, zpos]
        for a in range(arcs):
            part_rows = value[a * 8 : (a + 1) * 8]
            for t in range(full):
                at = (t * arcs + a) * 8
                out[zpos, at : at + 8, :] = part_rows[:, t * 128 : (t + 1) * 128]
            at = (full * arcs + a // 2) * 8
            lane0 = (a % 2) * rest
            out[zpos, at : at + 8, lane0 : lane0 + rest] = part_rows[:, full * 128 :]
        if arcs % 2:
            out[zpos, at : at + 8, rest:] = jnp.zeros((8, 128 - rest), jnp.float32)

    for copy in x_copies:
        copy.wait_send()

    order = []
    for n in range(depth - 1):
        down = depth - 1 - n
        down = down - (down <= z).astype(jnp.int32)
        up = n + (n >= z).astype(jnp.int32)
        order.append(jnp.where(2 * z < depth, down, up))
    order.append(z)
    y_dev = (x, (z * 2 + 1 - y) * 2 + core)
    tiles = ysend.shape[1] // 8
    cuts = [8 * (tiles * i // SPLIT) for i in range(SPLIT + 1)]
    pieces = [pl.ds(lo, hi - lo) for lo, hi in zip(cuts[:-1], cuts[1:])]
    y_copies = []
    for n, zpos in enumerate(order):
        finish(1 - y, zpos, ysend)
        for i, rows in enumerate(pieces):
            sem = n * SPLIT + i
            y_copies.append(
                remote(ysend.at[zpos, rows], yrecv.at[n, rows], y_send.at[sem], y_recv.at[sem], y_dev)
            )
    for zpos in order:
        finish(y, zpos, yown)
    z_copies = []
    for n, zpos in enumerate(order):
        for i, rows in enumerate(pieces):
            y_copies[n * SPLIT + i].wait()
            zsend[n, rows] = yown[zpos, rows] + yrecv[n, rows]
            if n < depth - 1:
                z_copies.append(
                    remote(
                        zsend.at[n, rows],
                        zrecv.at[z, rows],
                        z_send.at[n * SPLIT + i],
                        z_recv.at[z * SPLIT + i],
                        depth_dev(zpos),
                    )
                )
    for copy in z_copies:
        copy.wait_send()
    phase = zsend[depth - 1]
    for k in range(1, depth):
        zpos = (z + k) % depth
        for i, rows in enumerate(pieces):
            pltpu.make_async_remote_copy(
                src_ref=zsend.at[0, rows],
                dst_ref=zrecv.at[zpos, rows],
                send_sem=z_send.at[i],
                recv_sem=z_recv.at[zpos * SPLIT + i],
                device_id=depth_dev(zpos),
                device_id_type=MESH,
            ).wait_recv()
        phase = phase + zrecv[zpos]
    zsend[0] = phase
    for a in range(arcs):
        for q in range(PIXELS):
            lo = q * LENSLETS
            while lo < (q + 1) * LENSLETS:
                t = lo // 128
                hi = min((q + 1) * LENSLETS, (t + 1) * 128)
                if t < full:
                    at, lane0 = (t * arcs + a) * 8, lo - t * 128
                else:
                    at, lane0 = (full * arcs + a // 2) * 8, (a % 2) * rest + lo - t * 128
                to = a * LENSLETS + lo - q * LENSLETS
                phiq[q, :, to : to + hi - lo] = zsend[0, at : at + 8, lane0 : lane0 + hi - lo]
                lo = hi

    cosines, sines = [], []
    flux = None
    for q in range(PIXELS):
        amp = illq[q]
        phi = phiq[q]
        cosines.append(amp * jnp.cos(phi))
        sines.append(amp * jnp.sin(phi))
        flux = amp * amp if flux is None else flux + amp * amp
    tip = -float(PIXELS) * flux
    tilt = tip
    pix_row = lax.broadcasted_iota(jnp.int32, flux.shape, 0) % PIXELS
    for d in range(1, PIXELS):
        gain = pair_gain(d)
        even = -2.0 * PIXELS * (-1.0) ** d
        term = None
        for q in range(d, PIXELS):
            ch, sh, cl, sl = cosines[q], sines[q], cosines[q - d], sines[q - d]
            new = gain * (sh * cl - ch * sl) + even * (ch * cl + sh * sl)
            term = new if term is None else term + new
        tilt = tilt + term
        term = None
        for q in range(PIXELS):
            ch, sh = cosines[q], sines[q]
            cl, sl = pltpu.roll(ch, d, 0), pltpu.roll(sh, d, 0)
            new = gain * (sh * cl - ch * sl) + even * (ch * cl + sh * sl)
            term = new if term is None else term + new
        tip = tip + jnp.where(pix_row >= d, term, 0.0)
    for f in range(FRAMES):
        rows = slice(f * PIXELS, (f + 1) * PIXELS)
        total = jnp.sum(flux[rows], axis=0, keepdims=True) * (2.0 * PIXELS)
        for c, value in enumerate((tip, tilt)):
            slope = jnp.sum(value[rows], axis=0, keepdims=True) / total
            slopes_out[f, c : c + 1, :] = slope
            slope_sc[c, f : f + 1, :] = slope

    rec_copy.wait()
    rounded = [slope_sc[c].astype(jnp.bfloat16) for c in range(2)]
    tail = actuators - 6 * block

    def update(chip):
        def some(cols, width):
            value = jnp.dot(rounded[0], rec[0, :, cols], preferred_element_type=jnp.float32)
            value = value + jnp.dot(rounded[1], rec[1, :, cols], preferred_element_type=jnp.float32)
            upd[2 * chip] = value[:, :block]
            upd[2 * chip + 1, :, : width - block] = value[:, block:]

        @pl.when(chip < 3)
        def _():
            some(pl.ds(pl.multiple_of(chip * 2 * block, 128), 2 * block), 2 * block)

        @pl.when(chip == 3)
        def _():
            upd[7] = jnp.zeros_like(upd[7])
            some(slice(6 * block, actuators), tail)

    copies = []
    for n in range(7):
        to = slot(n)
        if n % 2 == 0:
            update(to // 2)
        copies.append(remote(upd.at[to], part.at[n], a_send.at[n], a_recv.at[n], plane(n)))
    for copy in copies:
        copy.wait()
    total = upd[me]
    for n in range(7):
        total = total + part[n]
    zsum[z] = total
    copies = []
    for k in range(1, depth):
        copies.append(
            remote(zsum.at[z], zsum.at[z], b_send.at[k - 1], b_recv.at[k - 1], depth_dev((z + k) % depth))
        )
    for copy in copies:
        copy.wait()
    total = zsum[0]
    for k in range(1, depth):
        total = total + zsum[k]
    limits = sat[me].astype(jnp.float32) * code_step
    first_cmd = jnp.clip(loop_gain * total[:1], -limits, limits)
    second_cmd = jnp.clip(first_cmd + loop_gain * total[1:], -limits, limits)
    part[0, :1] = first_cmd
    part[0, 1:] = second_cmd
    own_cols = pl.ds(pl.multiple_of(me * block, 128), block)
    upd_out[:, own_cols] = part[0]
    copies = []
    for n in range(7):
        copies.append(
            remote(upd_out.at[:, own_cols], upd_out.at[:, own_cols], c_send.at[n], c_recv.at[n], plane(n))
        )
    for copy in copies:
        copy.wait()


def fused_shards(screens, row_offset, col_offset, layer_bin, illumination, reconstructor, sat_code):
    layer_dev, rows_here, columns = screens.shape
    count_here = illumination.shape[1]
    actuators = reconstructor.shape[2]
    depth = lax.axis_size("strip") // 4
    arcs = count_here // LENSLETS
    chunk = (packed_rows(arcs), 128)
    rows = padded_rows(arcs)
    block = -(-actuators // (8 * 128)) * 128
    contraction = FRAMES * 2 * layer_dev * 2 * 2 * rows_here
    dma = pltpu.SemaphoreType.DMA
    spots = (FRAMES, GUIDE_STARS, row_offset.shape[1])
    vmem = pl.BlockSpec(memory_space=pltpu.VMEM)
    in_hbm = lambda v: pltpu.with_memory_space_constraint(v, pltpu.HBM)
    slopes, updates = pl.pallas_call(
        functools.partial(fused_kernel, depth, block),
        out_shape=(
            jax.ShapeDtypeStruct((FRAMES, 2, count_here), jnp.float32),
            jax.ShapeDtypeStruct((FRAMES, 8 * block), jnp.float32),
        ),
        in_specs=[pl.BlockSpec(memory_space=pltpu.HBM)] * 7,
        out_specs=(vmem, vmem),
        scratch_shapes=[
            pltpu.VMEM(screens.shape, jnp.bfloat16),
            pltpu.SMEM(spots, jnp.int32),
            pltpu.SMEM(spots, jnp.int32),
            pltpu.SMEM(layer_bin.shape, jnp.int32),
            pltpu.VMEM(illumination.shape, jnp.float32),
            pltpu.VMEM((2, 2 * layer_dev, rows_here, columns), jnp.float32),
            pltpu.VMEM((FRAMES, 2 * layer_dev, columns, PUPIL_PIX), jnp.bfloat16),
            pltpu.VMEM((2, depth * rows, contraction), jnp.bfloat16),
            pltpu.VMEM((contraction, PUPIL_PIX), jnp.bfloat16),
            pltpu.VMEM((2, depth, rows, PUPIL_PIX), jnp.float32),
            pltpu.VMEM((depth,) + chunk, jnp.float32),
            pltpu.VMEM((depth,) + chunk, jnp.float32),
            pltpu.VMEM((depth,) + chunk, jnp.float32),
            pltpu.VMEM((depth,) + chunk, jnp.float32),
            pltpu.VMEM((depth,) + chunk, jnp.float32),
            pltpu.VMEM((PIXELS, FRAMES * PIXELS, count_here), jnp.float32),
            pltpu.VMEM((PIXELS, FRAMES * PIXELS, count_here), jnp.float32),
            pltpu.VMEM((2, FRAMES, count_here), jnp.float32),
            pltpu.VMEM(reconstructor.shape, jnp.bfloat16),
            pltpu.VMEM((8, FRAMES, block), jnp.float32),
            pltpu.VMEM((7, FRAMES, block), jnp.float32),
            pltpu.VMEM((depth, FRAMES, block), jnp.float32),
            pltpu.VMEM((actuators,), jnp.int32),
            pltpu.VMEM((8, 1, block), jnp.int32),
            dma((5,)), dma, dma((layer_dev,)), dma((layer_dev,)), dma, dma, dma((layer_dev,)), dma((layer_dev,)),
            dma((depth * SPLIT,)), dma((depth * SPLIT,)),
            dma(((depth - 1) * SPLIT,)), dma((depth * SPLIT,)),
            dma((7,)), dma((7,)),
            dma((depth - 1,)), dma((depth - 1,)), dma,
            dma((7,)), dma((7,)),
        ],
        compiler_params=pltpu.CompilerParams(collective_id=0, has_side_effects=True, vmem_limit_bytes=44*2**20),
        name="fused",
    )(in_hbm(screens), in_hbm(row_offset.transpose(0, 2, 1)), in_hbm(col_offset.transpose(0, 2, 1)), in_hbm(layer_bin), in_hbm(illumination), in_hbm(reconstructor), in_hbm(sat_code))
    return slopes, updates[:, :actuators]


def solution(mesh):
    alt, strips = mesh.shape["alt"], mesh.shape["strip"]
    fused = alt == 2 == GUIDE_STARS and strips % 4 == 0 and strips > 4 and LENSLETS % strips == 0

    placed = (
        P("alt", "strip", None),
        P(),
        P(),
        P(),
        P(None, ("alt", "strip")),
        P(None, ("alt", "strip"), None),
        P(),
    )
    return jax.shard_map(
        fused_shards if fused else shards,
        mesh=mesh,
        in_specs=placed,
        out_specs=(P(None, None, ("alt", "strip")), P()),
        check_vma=False,
    )
```

```python
import functools
import math

import jax
import jax.numpy as jnp
from jax import lax
from jax.experimental import pallas as pl
from jax.experimental.pallas import tpu as pltpu
from jax.sharding import PartitionSpec as P

LENSLETS = 80
PIXELS = 4
GUIDE_STARS = 2
FRAMES = 2
ACTUATORS = 6000
PUPIL_PIX = 320
WINDOW = 384
SUBAPS_ALL = 12800


highest = lax.Precision.HIGHEST
loop_gain = 0.5
code_step = 0.125
bin_step = 0.03125


def bilinear(offsets):
    return jnp.maximum(0.0, 1.0 - jnp.abs(offsets))


def dft_tables():
    padded = 2 * PIXELS
    freq_index = jnp.arange(padded * padded, dtype=jnp.int32)
    freq_row = freq_index // padded
    freq_col = freq_index % padded
    pix_index = jnp.arange(PIXELS * PIXELS, dtype=jnp.int32)
    pix_row = pix_index // PIXELS
    pix_col = pix_index % PIXELS
    turn_count = (
        freq_row[:, None] * pix_row[None, :] + freq_col[:, None] * pix_col[None, :]
    ) % padded
    angles = turn_count.astype(jnp.float32) * (2.0 * math.pi / padded)
    coord_row = ((freq_row + PIXELS) % padded - PIXELS).astype(jnp.float32)
    coord_col = ((freq_col + PIXELS) % padded - PIXELS).astype(jnp.float32)
    return (jnp.cos(angles), jnp.sin(angles), coord_row, coord_col)


def centroids(pupil_phase, illumination, tables):
    cosine, sine_table, coord_row, coord_col = tables
    field_re = illumination * jnp.cos(pupil_phase)
    field_im = illumination * jnp.sin(pupil_phase)
    real_part = jnp.dot(cosine, field_re, precision=highest) + jnp.dot(
        sine_table, field_im, precision=highest
    )
    imag_part = jnp.dot(cosine, field_im, precision=highest) - jnp.dot(
        sine_table, field_re, precision=highest
    )
    intensity = real_part * real_part + imag_part * imag_part
    flux_sum = jnp.sum(intensity, axis=0)
    slope_row = jnp.sum(intensity * coord_row[:, None], axis=0) / flux_sum
    slope_col = jnp.sum(intensity * coord_col[:, None], axis=0) / flux_sum
    return jnp.stack([slope_row, slope_col])


def shards(screens, row_offset, col_offset, layer_bin, illumination, reconstructor, sat_code):
    layer_dev = screens.shape[0]
    rows_here = screens.shape[1]
    count_here = illumination.shape[1]
    group_pos = lax.axis_index("alt")
    strip_pos = lax.axis_index("strip")
    row_global = strip_pos * rows_here + jnp.arange(rows_here, dtype=jnp.int32)
    pupil_idx = jnp.arange(PUPIL_PIX, dtype=jnp.float32)
    window_idx = jnp.arange(WINDOW, dtype=jnp.float32)
    widened_layers = [
        jnp.pad(screens[layer_no], ((0, 0), (0, WINDOW))) for layer_no in range(layer_dev)
    ]
    frame_terms = []
    for frame_no in range(FRAMES):
        running = jnp.zeros((PIXELS, PIXELS, GUIDE_STARS, LENSLETS, LENSLETS), jnp.float32)
        for layer_no in range(layer_dev):
            layer_pos = group_pos * layer_dev + layer_no
            tops = lax.dynamic_index_in_dim(row_offset[frame_no], layer_pos, 0, keepdims=False)
            lefts = lax.dynamic_index_in_dim(col_offset[frame_no], layer_pos, 0, keepdims=False)
            bin_value = lax.dynamic_index_in_dim(layer_bin, layer_pos, 0, keepdims=False)
            shrink = 1.0 - bin_value.astype(jnp.float32) * bin_step
            col_weights = bilinear(window_idx[None, :] - pupil_idx[:, None] * shrink)
            widened = widened_layers[layer_no]

            def cut_columns(left_col):
                return lax.dynamic_slice_in_dim(widened, left_col, WINDOW, 1)

            strips = jax.vmap(cut_columns)(lefts).astype(jnp.float32)
            across = jnp.einsum("drc,jc->drj", strips, col_weights, precision=highest)
            offsets = (row_global[None, :] - tops[:, None]).astype(jnp.float32)
            row_weights = bilinear(offsets[:, None, :] - pupil_idx[None, :, None] * shrink)
            running = running + jnp.einsum(
                "dapr,drbq->pqdab",
                row_weights.reshape(GUIDE_STARS, LENSLETS, PIXELS, rows_here),
                across.reshape(GUIDE_STARS, rows_here, LENSLETS, PIXELS),
                precision=highest,
            )
        frame_terms.append(running.reshape(PIXELS * PIXELS, SUBAPS_ALL))
    phase_terms = jnp.concatenate(frame_terms, axis=0)
    partly = lax.psum_scatter(phase_terms, "alt", scatter_dimension=1, tiled=True)
    owned = lax.psum_scatter(partly, "strip", scatter_dimension=1, tiled=True)
    pupil_phase = owned.reshape(FRAMES, PIXELS * PIXELS, count_here)
    tables = dft_tables()
    slopes = jnp.stack(
        [centroids(pupil_phase[frame_no], illumination, tables) for frame_no in range(FRAMES)]
    )
    rounded = slopes.astype(jnp.bfloat16).reshape(FRAMES, 2 * count_here)
    partial_value = jnp.dot(
        rounded,
        reconstructor.reshape(2 * count_here, ACTUATORS),
        preferred_element_type=jnp.float32,
    )
    updates = lax.psum(partial_value, ("alt", "strip"))
    limits = sat_code.astype(jnp.float32) * code_step
    first_cmd = jnp.clip(loop_gain * updates[0], -limits, limits)
    second_cmd = jnp.clip(first_cmd + loop_gain * updates[1], -limits, limits)
    return (slopes, jnp.stack([first_cmd, second_cmd]))


MESH = pl.DeviceIdType.MESH
HALVES = 2
PLANES = 4
WIDE = -(-PUPIL_PIX // 128) * 128


def pair_gain(distance):
    turn = 2.0 * math.pi / (2 * PIXELS)
    return 4.0 * sum(k * math.sin(turn * k * distance) for k in range(1, PIXELS))


def padded_rows(arcs):
    return -(-arcs * FRAMES * PIXELS // 16) * 16


def tile_of(arcs, arc, part):
    full = PUPIL_PIX // 128
    pair = arc // 2 * (2 * full + 1)
    if part < full:
        return pair + arc % 2 * full + part
    return pair + (2 * full if arc // 2 * 2 + 1 < arcs else full)


def packed_tiles(arcs):
    return tile_of(arcs, arcs - 1, PUPIL_PIX // 128) + 1


def reaches(total, rows, first, last):
    for layer_bin in range(16):
        shrink = 1.0 - layer_bin * bin_step
        top = math.floor(total - 1 - (PUPIL_PIX - 1) * shrink)
        if top + last * shrink > rows[0] - 1 and first * shrink < rows[1] + 1:
            return True
    return False


def far_pattern(total, arcs):
    plane_rows = total // PLANES
    strip_rows = arcs * PIXELS
    for strip in range(4):
        first = strip * strip_rows
        if reaches(total, (total - plane_rows, total - 1), first, first + strip_rows - 1):
            return False
        first += (PLANES - 1) * 4 * strip_rows
        low = first + 2 * PIXELS if strip == 0 else first
        if reaches(total, (0, plane_rows - 1), low, first + strip_rows - 1):
            return False
    return True


def fused_kernel(
    block,
    scr_hbm,
    row_hbm,
    col_hbm,
    bin_hbm,
    ill_hbm,
    rec_hbm,
    sat_hbm,
    slopes_out,
    upd_out,
    scr_ref,
    row_ref,
    col_ref,
    bin_ref,
    ill_ref,
    scr_all,
    colw,
    roww,
    rhs,
    acc,
    part,
    relay_in,
    main_in,
    far_in,
    phase_sc,
    phiq,
    illq,
    slope_sc,
    rec,
    upd,
    gathered,
    zsum,
    sat_raw,
    sat,
    in_sem,
    rec_sem,
    sat_sem,
    own_send,
    own_recv,
    pass_send,
    pass_recv,
    core_send,
    core_recv,
    ra_send,
    ra_recv,
    m_send,
    m_recv,
    far_send,
    far_recv,
    credit,
    a_send,
    a_recv,
    b_send,
    b_recv,
    c_send,
    c_recv,
):
    layer_dev, rows_here, columns = scr_ref.shape
    count_here = ill_ref.shape[1]
    arcs = count_here // LENSLETS
    chunk_rows = padded_rows(arcs)
    depth = PLANES
    full = PUPIL_PIX // 128
    rest = PUPIL_PIX - full * 128
    actuators = rec_hbm.shape[2]

    loads = [
        pltpu.make_async_copy(src, dst, in_sem.at[n])
        for n, (src, dst) in enumerate(
            (
                (scr_hbm, scr_ref),
                (row_hbm, row_ref),
                (col_hbm, col_ref),
                (bin_hbm, bin_ref),
                (ill_hbm, ill_ref),
            )
        )
    ]
    for load in loads:
        load.start()
    rec_copy = pltpu.make_async_copy(rec_hbm, rec, rec_sem)
    rec_copy.start()
    sat_load = pltpu.make_async_copy(sat_hbm, sat_raw, sat_sem)
    sat_load.start()

    x = lax.axis_index("alt")
    strip = lax.axis_index("strip")
    core = strip % 2
    y = (strip // 2) % 2
    z = strip // 4
    me = (x * 2 + y) * 2 + core

    offsets = ((1, 1, 0), (1, 1, 1), (1, 0, 0), (1, 0, 1), (0, 1, 0), (0, 1, 1), (0, 0, 1))

    def place(n):
        dx, dy, dc = offsets[n]
        return ((x + dx) % 2, (y + dy) % 2, (core + dc) % 2)

    def plane(n):
        px, py, pc = place(n)
        return (px, (z * 2 + py) * 2 + pc)

    def slot(n):
        px, py, pc = place(n)
        return (px * 2 + py) * 2 + pc

    def depth_dev(zpos):
        return (x, (zpos * 2 + y) * 2 + core)

    x_dev = (1 - x, strip)
    y_dev = (x, (z * 2 + 1 - y) * 2 + core)
    core_dev = (x, (z * 2 + y) * 2 + 1 - core)
    low_end = z == 0
    high_end = z == depth - 1
    outer = low_end | high_end
    corner = (y == 0) & (core == 0)

    barrier = pltpu.get_barrier_semaphore()
    for device in (x_dev, y_dev, core_dev):
        pl.semaphore_signal(barrier, inc=1, device_id=device, device_id_type=MESH)

    @pl.when(jnp.logical_not(low_end))
    def _():
        pl.semaphore_signal(barrier, inc=1, device_id=depth_dev(z - 1), device_id_type=MESH)

    @pl.when(jnp.logical_not(high_end))
    def _():
        pl.semaphore_signal(barrier, inc=1, device_id=depth_dev(z + 1), device_id_type=MESH)

    spot = y * 2 + core
    other = (1 - y) * 2 + core
    loads[0].wait()
    for li in range(layer_dev):
        scr_all[x * layer_dev + li, spot] = scr_ref[li].astype(jnp.float32)

    @pl.when(outer)
    def _():
        pl.semaphore_wait(barrier, 4)

    @pl.when(jnp.logical_not(outer))
    def _():
        pl.semaphore_wait(barrier, 5)

    def remote(src, dst, send, recv, device):
        copy = pltpu.make_async_remote_copy(
            src_ref=src, dst_ref=dst, send_sem=send, recv_sem=recv, device_id=device, device_id_type=MESH
        )
        copy.start()
        return copy

    half = rows_here // HALVES

    def piece(layer, at, h):
        return scr_all.at[layer, at, pl.ds(h * half, half)]

    def share(which, li, h, device):
        n = (which * layer_dev + li) * HALVES + h
        here = piece(x * layer_dev + li, spot, h)
        return remote(here, here, own_send.at[n], own_recv.at[n], device)

    x_copies, y_copies = {}, {}
    for step in range(layer_dev):
        for h in range(HALVES):
            x_copies[step, h] = share(0, step, h, x_dev)
            y_copies[layer_dev - 1 - step, h] = share(1, layer_dev - 1 - step, h, y_dev)
    core_copies = []

    def to_core(here):
        n = len(core_copies)
        core_copies.append(remote(here, here, core_send.at[n], core_recv.at[n], core_dev))

    to_core(scr_all.at[x * layer_dev, spot])
    to_core(scr_all.at[x * layer_dev + 1, spot])

    @pl.when((z == 1) & corner)
    def _():
        pl.semaphore_signal(credit, inc=1, device_id=depth_dev(z - 1), device_id_type=MESH)

    for load in loads[1:]:
        load.wait()

    layers = [((x + rel) % 2) * layer_dev + li for rel in range(2) for li in range(layer_dev)]
    shrinks = [1.0 - bin_ref[layer].astype(jnp.float32) * bin_step for layer in layers]
    tops = [[row_ref[f, x, layer].astype(jnp.float32) for layer in layers] for f in range(FRAMES)]
    lefts = [[col_ref[f, x, layer].astype(jnp.float32) for layer in layers] for f in range(FRAMES)]

    width = colw.shape[2]
    col_pos = lax.broadcasted_iota(jnp.int32, (columns, width), 0).astype(jnp.float32)
    lane = lax.broadcasted_iota(jnp.int32, (1, width), 1)
    second = lane >= WIDE
    lane = jnp.where(second, lane - WIDE, lane)
    q_of = (
        (lane >= LENSLETS).astype(jnp.int32)
        + (lane >= 2 * LENSLETS).astype(jnp.int32)
        + (lane >= 3 * LENSLETS).astype(jnp.int32)
    )
    pupil_col = ((lane - q_of * LENSLETS) * PIXELS + q_of).astype(jnp.float32)

    def column_weights(n):
        start = pupil_col * shrinks[n] + jnp.where(second, lefts[1][n], lefts[0][n])
        colw[n] = bilinear(col_pos - start).astype(jnp.bfloat16)

    mine = range(layer_dev)
    theirs = range(layer_dev, 2 * layer_dev)
    pair = 2 * rows_here
    stages = (
        (mine, 2 * y, pair),
        (theirs, 2 * y, pair),
        (mine, 2 * (1 - y), pair),
        (theirs, other, rows_here),
        (theirs, 2 * (1 - y) + 1 - core, rows_here),
    )
    begins = [0]
    for members, at, rows in stages:
        begins.append(begins[-1] + len(members) * FRAMES * 2 * rows)

    def row_weights(number):
        members, at, rows = stages[number]
        seg = 2 * rows
        row_pos = lax.broadcasted_iota(jnp.int32, (chunk_rows, seg), 1) % rows + (z * 4 + at) * rows_here
        row_pos = row_pos.astype(jnp.float32)
        row_sub = lax.broadcasted_iota(jnp.int32, (chunk_rows, seg), 0)
        row_base = row_sub // 8 * PIXELS + row_sub % PIXELS
        row_frame = row_sub // PIXELS % FRAMES
        for zpos in range(depth):
            pupil_row = (row_base + ((zpos * 2 + y) * 2 + core) * (arcs * PIXELS)).astype(jnp.float32)
            for i, n in enumerate(members):
                reach = pupil_row * shrinks[n]
                for f in range(FRAMES):
                    weight = jnp.where(row_frame == f, bilinear(row_pos - tops[f][n] - reach), 0.0)
                    lo = begins[number] + (i * FRAMES + f) * seg
                    roww[zpos * chunk_rows : (zpos + 1) * chunk_rows, lo : lo + seg] = weight.astype(jnp.bfloat16)

    def across(number, n):
        members, at, rows = stages[number]
        blocks = rows // rows_here
        source = scr_all[layers[n], pl.ds(at, blocks)].reshape(rows, columns).astype(jnp.bfloat16)
        value = jnp.dot(source, colw[n], preferred_element_type=jnp.float32)
        for f in range(FRAMES):
            one = value[:, f * WIDE : f * WIDE + PUPIL_PIX]
            high = one.astype(jnp.bfloat16)
            low = (one - high.astype(jnp.float32)).astype(jnp.bfloat16)
            lo = begins[number] + ((n - members[0]) * FRAMES + f) * 2 * rows
            rhs[lo : lo + rows, :] = high
            rhs[lo + rows : lo + 2 * rows, :] = low

    def project(number):
        lo, hi = begins[number], begins[number + 1]
        return jnp.dot(roww[:, lo:hi], rhs[lo:hi, :], preferred_element_type=jnp.float32)

    for n in range(2 * layer_dev):
        column_weights(n)
    for number in range(len(stages)):
        row_weights(number)

    passed = {}

    def pass_on(which, h, here, device):
        n = which * HALVES + h
        passed[which, h] = remote(here, here, pass_send.at[n], pass_recv.at[n], device)

    for h in range(HALVES):
        here = piece((1 - x) * layer_dev, spot, h)
        x_copies[0, h].wait_recv()
        pass_on(0, h, here, y_dev)
        to_core(here)
        here = piece(x * layer_dev + 1, other, h)
        y_copies[1, h].wait_recv()
        pass_on(1, h, here, x_dev)
        to_core(here)
    for copy in core_copies[:2]:
        copy.wait()
    for n in mine:
        across(0, n)
    acc[...] = project(0)
    for p in range(PIXELS):
        for q in range(PIXELS):
            for f in range(FRAMES):
                illq[q, f * PIXELS + p : f * PIXELS + p + 1, :] = ill_ref[p * PIXELS + q : p * PIXELS + q + 1, :]
    sat_load.wait()
    for n in range(8):
        some = min(block, actuators - n * block)
        sat[n, 0, :some] = sat_raw[n * block : n * block + some]
    for h in range(HALVES):
        x_copies[1, h].wait_recv()
        to_core(piece((1 - x) * layer_dev + 1, spot, h))
        y_copies[0, h].wait_recv()
        to_core(piece(x * layer_dev, other, h))
    for copy in core_copies[2 : 2 + 2 * HALVES]:
        copy.wait()
    across(1, layer_dev)
    across(2, 1)
    for copy in core_copies[2 + 2 * HALVES : 2 + 4 * HALVES]:
        copy.wait()
    across(1, layer_dev + 1)
    across(2, 0)
    for h in range(HALVES):
        passed[0, h].wait_recv()
        to_core(piece((1 - x) * layer_dev, other, h))
        passed[1, h].wait_recv()
        to_core(piece((1 - x) * layer_dev + 1, other, h))
    acc[...] += project(1) + project(2)
    for n in theirs:
        across(3, n)
    acc[...] += project(3)
    for copy in core_copies[2 + 4 * HALVES :]:
        copy.wait()
    for n in theirs:
        across(4, n)
    acc[...] += project(4)
    for copy in list(x_copies.values()) + list(y_copies.values()) + list(passed.values()):
        copy.wait_send()

    def pack(zpos):
        value = acc[pl.ds(pl.multiple_of(zpos * chunk_rows, chunk_rows), chunk_rows), :]
        for a in range(arcs):
            lines = value[a * 8 : (a + 1) * 8]
            for t in range(full):
                at = tile_of(arcs, a, t) * 8
                part[zpos, at : at + 8, :] = lines[:, t * 128 : (t + 1) * 128]
            at = tile_of(arcs, a, full) * 8
            lane0 = a % 2 * rest
            part[zpos, at : at + 8, lane0 : lane0 + rest] = lines[:, full * 128 :]
        if arcs % 2:
            at = tile_of(arcs, arcs - 1, full) * 8
            part[zpos, at : at + 8, rest:] = jnp.zeros((8, 128 - rest), jnp.float32)

    edge = tile_of(arcs, 1, full) + 1
    tiles = packed_tiles(arcs)
    pieces = [pl.ds(edge * 8, (tiles - edge) * 8), pl.ds(0, edge * 8)]
    count = len(pieces)
    below = z < depth // 2
    ahead = jnp.where(below, 1, -1)
    side = jnp.where(below, 0, 1)
    pack(z + 2 * ahead)
    first_copies = []
    for i, rows in enumerate(pieces):
        first_copies.append(
            remote(
                part.at[z + 2 * ahead, rows],
                relay_in.at[side, rows],
                ra_send.at[i],
                ra_recv.at[side * count + i],
                depth_dev(z + ahead),
            )
        )

    def relay_wait(s, i):
        pltpu.make_async_remote_copy(
            src_ref=part.at[0, pieces[i]],
            dst_ref=relay_in.at[s, pieces[i]],
            send_sem=ra_send.at[i],
            recv_sem=ra_recv.at[s * count + i],
            device_id=depth_dev(z),
            device_id_type=MESH,
        ).wait_recv()

    def main_copy(s, i, zpos):
        return pltpu.make_async_remote_copy(
            src_ref=part.at[zpos, pieces[i]],
            dst_ref=main_in.at[s, pieces[i]],
            send_sem=m_send.at[s * count + i],
            recv_sem=m_recv.at[s * count + i],
            device_id=depth_dev(zpos),
            device_id_type=MESH,
        )

    far_copy = pltpu.make_async_remote_copy(
        src_ref=part.at[depth - 1, pieces[1]],
        dst_ref=far_in,
        send_sem=far_send,
        recv_sem=far_recv,
        device_id=depth_dev(2),
        device_id_type=MESH,
    )

    @pl.when(outer)
    def _():
        pack(z + ahead)
        copies = []
        for i in range(count):
            copies.append(main_copy(side, i, z + ahead))
            copies[-1].start()

        @pl.when(low_end & corner)
        def _():
            pack(depth - 1)
            pl.semaphore_wait(credit, 1)
            far_copy.start()
            far_copy.wait_send()

        pack(z)
        for i, rows in enumerate(pieces):
            main_copy(1 - side, i, z + ahead).wait_recv()
            phase_sc[rows] = part[z, rows] + main_in[1 - side, rows]
        for copy in copies:
            copy.wait_send()

    @pl.when(jnp.logical_not(outer))
    def _():
        pack(z + 1)
        pack(z - 1)
        copies = []
        for i, rows in enumerate(pieces):
            for s in range(2):
                to = z + 1 - 2 * s
                relay_wait(s, i)
                if i == 1 and s == 0:

                    @pl.when((z == 2) & corner)
                    def _():
                        far_copy.wait_recv()
                        part[depth - 1, rows] = part[depth - 1, rows] + far_in[...]

                part[to, rows] = part[to, rows] + relay_in[s, rows]
                copies.append(main_copy(s, i, to))
                copies[-1].start()
        pack(z)
        for i, rows in enumerate(pieces):
            for s in range(2):
                main_copy(s, i, z + 1 - 2 * s).wait_recv()
            phase_sc[rows] = part[z, rows] + main_in[0, rows] + main_in[1, rows]
        for copy in copies:
            copy.wait_send()

    for copy in first_copies:
        copy.wait_send()

    for a in range(arcs):
        for q in range(PIXELS):
            lo = q * LENSLETS
            while lo < (q + 1) * LENSLETS:
                t = lo // 128
                hi = min((q + 1) * LENSLETS, (t + 1) * 128)
                at = tile_of(arcs, a, t) * 8
                lane0 = lo - t * 128 + (a % 2 * rest if t == full else 0)
                to = a * LENSLETS + lo - q * LENSLETS
                phiq[q, :, to : to + hi - lo] = phase_sc[at : at + 8, lane0 : lane0 + hi - lo]
                lo = hi

    cosines, sines = [], []
    flux = None
    for q in range(PIXELS):
        amp = illq[q]
        phi = phiq[q]
        cosines.append(amp * jnp.cos(phi))
        sines.append(amp * jnp.sin(phi))
        flux = amp * amp if flux is None else flux + amp * amp
    tip = -float(PIXELS) * flux
    tilt = tip
    pix_row = lax.broadcasted_iota(jnp.int32, flux.shape, 0) % PIXELS
    for d in range(1, PIXELS):
        gain = pair_gain(d)
        even = -2.0 * PIXELS * (-1.0) ** d
        term = None
        for q in range(d, PIXELS):
            ch, sh, cl, sl = cosines[q], sines[q], cosines[q - d], sines[q - d]
            new = gain * (sh * cl - ch * sl) + even * (ch * cl + sh * sl)
            term = new if term is None else term + new
        tilt = tilt + term
        term = None
        for q in range(PIXELS):
            ch, sh = cosines[q], sines[q]
            cl, sl = pltpu.roll(ch, d, 0), pltpu.roll(sh, d, 0)
            new = gain * (sh * cl - ch * sl) + even * (ch * cl + sh * sl)
            term = new if term is None else term + new
        tip = tip + jnp.where(pix_row >= d, term, 0.0)
    for f in range(FRAMES):
        rows = slice(f * PIXELS, (f + 1) * PIXELS)
        total = jnp.sum(flux[rows], axis=0, keepdims=True) * (2.0 * PIXELS)
        for c, value in enumerate((tip, tilt)):
            slope = jnp.sum(value[rows], axis=0, keepdims=True) / total
            slopes_out[f, c : c + 1, :] = slope
            slope_sc[c, f : f + 1, :] = slope

    rec_copy.wait()
    rounded = [slope_sc[c].astype(jnp.bfloat16) for c in range(2)]
    tail = actuators - 6 * block

    def update(chip):
        def some(cols, width):
            value = jnp.dot(rounded[0], rec[0, :, cols], preferred_element_type=jnp.float32)
            value = value + jnp.dot(rounded[1], rec[1, :, cols], preferred_element_type=jnp.float32)
            upd[2 * chip] = value[:, :block]
            upd[2 * chip + 1, :, : width - block] = value[:, block:]

        @pl.when(chip < 3)
        def _():
            some(pl.ds(pl.multiple_of(chip * 2 * block, 128), 2 * block), 2 * block)

        @pl.when(chip == 3)
        def _():
            upd[7] = jnp.zeros_like(upd[7])
            some(slice(6 * block, actuators), tail)

    copies = []
    for n in range(7):
        to = slot(n)
        if n % 2 == 0:
            update(to // 2)
        copies.append(remote(upd.at[to], gathered.at[n], a_send.at[n], a_recv.at[n], plane(n)))
    for copy in copies:
        copy.wait()
    total = upd[me]
    for n in range(7):
        total = total + gathered[n]
    zsum[z] = total
    copies = []
    for k in range(1, depth):
        copies.append(
            remote(zsum.at[z], zsum.at[z], b_send.at[k - 1], b_recv.at[k - 1], depth_dev((z + k) % depth))
        )
    for copy in copies:
        copy.wait()
    total = zsum[0]
    for k in range(1, depth):
        total = total + zsum[k]
    limits = sat[me].astype(jnp.float32) * code_step
    first_cmd = jnp.clip(loop_gain * total[:1], -limits, limits)
    second_cmd = jnp.clip(first_cmd + loop_gain * total[1:], -limits, limits)
    gathered[0, :1] = first_cmd
    gathered[0, 1:] = second_cmd
    own_cols = pl.ds(pl.multiple_of(me * block, 128), block)
    upd_out[:, own_cols] = gathered[0]
    copies = []
    for n in range(7):
        copies.append(
            remote(upd_out.at[:, own_cols], upd_out.at[:, own_cols], c_send.at[n], c_recv.at[n], plane(n))
        )
    for copy in copies:
        copy.wait()


def fused_shards(screens, row_offset, col_offset, layer_bin, illumination, reconstructor, sat_code):
    layer_dev, rows_here, columns = screens.shape
    count_here = illumination.shape[1]
    actuators = reconstructor.shape[2]
    depth = PLANES
    arcs = count_here // LENSLETS
    chunk = (packed_tiles(arcs) * 8, 128)
    edge = ((tile_of(arcs, 1, PUPIL_PIX // 128) + 1) * 8, 128)
    rows = padded_rows(arcs)
    block = -(-actuators // (8 * 128)) * 128
    contraction = FRAMES * 2 * 2 * layer_dev * 4 * rows_here
    width = (FRAMES - 1) * WIDE + PUPIL_PIX
    dma = pltpu.SemaphoreType.DMA
    spots = (FRAMES, GUIDE_STARS, row_offset.shape[1])
    vmem = pl.BlockSpec(memory_space=pltpu.VMEM)

    def in_hbm(value):
        return pltpu.with_memory_space_constraint(value, pltpu.HBM)

    slopes, updates = pl.pallas_call(
        functools.partial(fused_kernel, block),
        out_shape=(
            jax.ShapeDtypeStruct((FRAMES, 2, count_here), jnp.float32),
            jax.ShapeDtypeStruct((FRAMES, 8 * block), jnp.float32),
        ),
        in_specs=[pl.BlockSpec(memory_space=pltpu.HBM)] * 7,
        out_specs=(vmem, vmem),
        scratch_shapes=[
            pltpu.VMEM(screens.shape, jnp.bfloat16),
            pltpu.SMEM(spots, jnp.int32),
            pltpu.SMEM(spots, jnp.int32),
            pltpu.SMEM(layer_bin.shape, jnp.int32),
            pltpu.VMEM(illumination.shape, jnp.float32),
            pltpu.VMEM((2 * layer_dev, 4, rows_here, columns), jnp.float32),
            pltpu.VMEM((2 * layer_dev, columns, width), jnp.bfloat16),
            pltpu.VMEM((depth * rows, contraction), jnp.bfloat16),
            pltpu.VMEM((contraction, PUPIL_PIX), jnp.bfloat16),
            pltpu.VMEM((depth * rows, PUPIL_PIX), jnp.float32),
            pltpu.VMEM((depth,) + chunk, jnp.float32),
            pltpu.VMEM((2,) + chunk, jnp.float32),
            pltpu.VMEM((2,) + chunk, jnp.float32),
            pltpu.VMEM(edge, jnp.float32),
            pltpu.VMEM(chunk, jnp.float32),
            pltpu.VMEM((PIXELS, FRAMES * PIXELS, count_here), jnp.float32),
            pltpu.VMEM((PIXELS, FRAMES * PIXELS, count_here), jnp.float32),
            pltpu.VMEM((2, FRAMES, count_here), jnp.float32),
            pltpu.VMEM(reconstructor.shape, jnp.bfloat16),
            pltpu.VMEM((8, FRAMES, block), jnp.float32),
            pltpu.VMEM((7, FRAMES, block), jnp.float32),
            pltpu.VMEM((depth, FRAMES, block), jnp.float32),
            pltpu.VMEM((actuators,), jnp.int32),
            pltpu.VMEM((8, 1, block), jnp.int32),
            dma((5,)), dma, dma,
            dma((2 * layer_dev * HALVES,)), dma((2 * layer_dev * HALVES,)),
            dma((2 * HALVES,)), dma((2 * HALVES,)),
            dma((2 + 6 * HALVES,)), dma((2 + 6 * HALVES,)),
            dma((2,)), dma((4,)), dma((4,)), dma((4,)), dma, dma,
            pltpu.SemaphoreType.REGULAR,
            dma((7,)), dma((7,)),
            dma((depth - 1,)), dma((depth - 1,)),
            dma((7,)), dma((7,)),
        ],
        compiler_params=pltpu.CompilerParams(collective_id=0, has_side_effects=True, vmem_limit_bytes=44 * 2**20),
        name="fused",
    )(
        in_hbm(screens),
        in_hbm(row_offset.transpose(0, 2, 1)),
        in_hbm(col_offset.transpose(0, 2, 1)),
        in_hbm(layer_bin),
        in_hbm(illumination),
        in_hbm(reconstructor),
        in_hbm(sat_code),
    )
    return slopes, updates[:, :actuators]


def step(screens, row_offset, col_offset, layer_bin, illumination, reconstructor, sat_code):
    strips = lax.axis_size("strip")
    fused = (
        lax.axis_size("alt") == 2 == GUIDE_STARS
        and strips == 4 * PLANES
        and screens.shape[0] == 2
        and LENSLETS % strips == 0
        and LENSLETS // strips > 2
        and screens.shape[1] % 16 == 0
        and far_pattern(strips * screens.shape[1], LENSLETS // strips)
    )
    chosen = fused_shards if fused else shards
    return chosen(screens, row_offset, col_offset, layer_bin, illumination, reconstructor, sat_code)


def solution(mesh):
    placed = (
        P("alt", "strip", None),
        P(),
        P(),
        P(),
        P(None, ("alt", "strip")),
        P(None, ("alt", "strip"), None),
        P(),
    )
    return jax.shard_map(
        step,
        mesh=mesh,
        in_specs=placed,
        out_specs=(P(None, None, ("alt", "strip")), P()),
        check_vma=False,
    )
```

```python
import functools
import math

import jax
import jax.numpy as jnp
from jax import lax
from jax.experimental import pallas as pl
from jax.experimental.pallas import tpu as pltpu
from jax.sharding import PartitionSpec as P

LENSLETS = 80
PIXELS = 4
GUIDE_STARS = 2
FRAMES = 2
ACTUATORS = 6000
PUPIL_PIX = 320
WINDOW = 384
SUBAPS_ALL = 12800


highest = lax.Precision.HIGHEST
loop_gain = 0.5
code_step = 0.125
bin_step = 0.03125


def bilinear(offsets):
    return jnp.maximum(0.0, 1.0 - jnp.abs(offsets))


def dft_tables():
    padded = 2 * PIXELS
    freq_index = jnp.arange(padded * padded, dtype=jnp.int32)
    freq_row = freq_index // padded
    freq_col = freq_index % padded
    pix_index = jnp.arange(PIXELS * PIXELS, dtype=jnp.int32)
    pix_row = pix_index // PIXELS
    pix_col = pix_index % PIXELS
    turn_count = (
        freq_row[:, None] * pix_row[None, :] + freq_col[:, None] * pix_col[None, :]
    ) % padded
    angles = turn_count.astype(jnp.float32) * (2.0 * math.pi / padded)
    coord_row = ((freq_row + PIXELS) % padded - PIXELS).astype(jnp.float32)
    coord_col = ((freq_col + PIXELS) % padded - PIXELS).astype(jnp.float32)
    return (jnp.cos(angles), jnp.sin(angles), coord_row, coord_col)


def centroids(pupil_phase, illumination, tables):
    cosine, sine_table, coord_row, coord_col = tables
    field_re = illumination * jnp.cos(pupil_phase)
    field_im = illumination * jnp.sin(pupil_phase)
    real_part = jnp.dot(cosine, field_re, precision=highest) + jnp.dot(
        sine_table, field_im, precision=highest
    )
    imag_part = jnp.dot(cosine, field_im, precision=highest) - jnp.dot(
        sine_table, field_re, precision=highest
    )
    intensity = real_part * real_part + imag_part * imag_part
    flux_sum = jnp.sum(intensity, axis=0)
    slope_row = jnp.sum(intensity * coord_row[:, None], axis=0) / flux_sum
    slope_col = jnp.sum(intensity * coord_col[:, None], axis=0) / flux_sum
    return jnp.stack([slope_row, slope_col])


def shards(screens, row_offset, col_offset, layer_bin, illumination, reconstructor, sat_code):
    layer_dev = screens.shape[0]
    rows_here = screens.shape[1]
    count_here = illumination.shape[1]
    group_pos = lax.axis_index("alt")
    strip_pos = lax.axis_index("strip")
    row_global = strip_pos * rows_here + jnp.arange(rows_here, dtype=jnp.int32)
    pupil_idx = jnp.arange(PUPIL_PIX, dtype=jnp.float32)
    window_idx = jnp.arange(WINDOW, dtype=jnp.float32)
    widened_layers = [
        jnp.pad(screens[layer_no], ((0, 0), (0, WINDOW))) for layer_no in range(layer_dev)
    ]
    frame_terms = []
    for frame_no in range(FRAMES):
        running = jnp.zeros((PIXELS, PIXELS, GUIDE_STARS, LENSLETS, LENSLETS), jnp.float32)
        for layer_no in range(layer_dev):
            layer_pos = group_pos * layer_dev + layer_no
            tops = lax.dynamic_index_in_dim(row_offset[frame_no], layer_pos, 0, keepdims=False)
            lefts = lax.dynamic_index_in_dim(col_offset[frame_no], layer_pos, 0, keepdims=False)
            bin_value = lax.dynamic_index_in_dim(layer_bin, layer_pos, 0, keepdims=False)
            shrink = 1.0 - bin_value.astype(jnp.float32) * bin_step
            col_weights = bilinear(window_idx[None, :] - pupil_idx[:, None] * shrink)
            widened = widened_layers[layer_no]

            def cut_columns(left_col):
                return lax.dynamic_slice_in_dim(widened, left_col, WINDOW, 1)

            strips = jax.vmap(cut_columns)(lefts).astype(jnp.float32)
            across = jnp.einsum("drc,jc->drj", strips, col_weights, precision=highest)
            offsets = (row_global[None, :] - tops[:, None]).astype(jnp.float32)
            row_weights = bilinear(offsets[:, None, :] - pupil_idx[None, :, None] * shrink)
            running = running + jnp.einsum(
                "dapr,drbq->pqdab",
                row_weights.reshape(GUIDE_STARS, LENSLETS, PIXELS, rows_here),
                across.reshape(GUIDE_STARS, rows_here, LENSLETS, PIXELS),
                precision=highest,
            )
        frame_terms.append(running.reshape(PIXELS * PIXELS, SUBAPS_ALL))
    phase_terms = jnp.concatenate(frame_terms, axis=0)
    partly = lax.psum_scatter(phase_terms, "alt", scatter_dimension=1, tiled=True)
    owned = lax.psum_scatter(partly, "strip", scatter_dimension=1, tiled=True)
    pupil_phase = owned.reshape(FRAMES, PIXELS * PIXELS, count_here)
    tables = dft_tables()
    slopes = jnp.stack(
        [centroids(pupil_phase[frame_no], illumination, tables) for frame_no in range(FRAMES)]
    )
    rounded = slopes.astype(jnp.bfloat16).reshape(FRAMES, 2 * count_here)
    partial_value = jnp.dot(
        rounded,
        reconstructor.reshape(2 * count_here, ACTUATORS),
        preferred_element_type=jnp.float32,
    )
    updates = lax.psum(partial_value, ("alt", "strip"))
    limits = sat_code.astype(jnp.float32) * code_step
    first_cmd = jnp.clip(loop_gain * updates[0], -limits, limits)
    second_cmd = jnp.clip(first_cmd + loop_gain * updates[1], -limits, limits)
    return (slopes, jnp.stack([first_cmd, second_cmd]))


MESH = pl.DeviceIdType.MESH
HALVES = 1
PLANES = 4
WIDE = -(-PUPIL_PIX // 128) * 128


def pair_gain(distance):
    turn = 2.0 * math.pi / (2 * PIXELS)
    return 4.0 * sum(k * math.sin(turn * k * distance) for k in range(1, PIXELS))


def padded_rows(arcs):
    return -(-arcs * FRAMES * PIXELS // 16) * 16


def tile_of(arcs, arc, part):
    full = PUPIL_PIX // 128
    pair = arc // 2 * (2 * full + 1)
    if part < full:
        return pair + arc % 2 * full + part
    return pair + (2 * full if arc // 2 * 2 + 1 < arcs else full)


def packed_tiles(arcs):
    return tile_of(arcs, arcs - 1, PUPIL_PIX // 128) + 1


def reaches(total, rows, first, last):
    for layer_bin in range(16):
        shrink = 1.0 - layer_bin * bin_step
        top = math.floor(total - 1 - (PUPIL_PIX - 1) * shrink)
        if top + last * shrink > rows[0] - 1 and first * shrink < rows[1] + 1:
            return True
    return False


def far_pattern(total, arcs):
    plane_rows = total // PLANES
    strip_rows = arcs * PIXELS
    for strip in range(4):
        first = strip * strip_rows
        if reaches(total, (total - plane_rows, total - 1), first, first + strip_rows - 1):
            return False
        first += (PLANES - 1) * 4 * strip_rows
        low = first + 2 * PIXELS if strip == 0 else first
        if reaches(total, (0, plane_rows - 1), low, first + strip_rows - 1):
            return False
    return True


def fused_kernel(
    block,
    scr_hbm,
    row_hbm,
    col_hbm,
    bin_hbm,
    ill_hbm,
    rec_hbm,
    sat_hbm,
    slopes_out,
    upd_out,
    scr_ref,
    row_ref,
    col_ref,
    bin_ref,
    ill_ref,
    scr_all,
    colw,
    roww,
    rhs,
    acc,
    part,
    z_in,
    far_in,
    phase_sc,
    phiq,
    illq,
    slope_sc,
    rec,
    upd,
    gathered,
    zsum,
    sat_raw,
    sat,
    in_sem,
    rec_sem,
    sat_sem,
    own_send,
    own_recv,
    pass_send,
    pass_recv,
    core_send,
    core_recv,
    z_send,
    z_recv,
    far_send,
    far_recv,
    credit,
    a_send,
    a_recv,
    b_send,
    b_recv,
    c_send,
    c_recv,
):
    layer_dev, rows_here, columns = scr_ref.shape
    count_here = ill_ref.shape[1]
    arcs = count_here // LENSLETS
    chunk_rows = padded_rows(arcs)
    depth = PLANES
    full = PUPIL_PIX // 128
    rest = PUPIL_PIX - full * 128
    actuators = rec_hbm.shape[2]

    loads = [
        pltpu.make_async_copy(src, dst, in_sem.at[n])
        for n, (src, dst) in enumerate(
            (
                (scr_hbm, scr_ref),
                (row_hbm, row_ref),
                (col_hbm, col_ref),
                (bin_hbm, bin_ref),
                (ill_hbm, ill_ref),
            )
        )
    ]
    for load in loads:
        load.start()
    rec_copy = pltpu.make_async_copy(rec_hbm, rec, rec_sem)
    rec_copy.start()
    sat_load = pltpu.make_async_copy(sat_hbm, sat_raw, sat_sem)
    sat_load.start()

    x = lax.axis_index("alt")
    strip = lax.axis_index("strip")
    core = strip % 2
    y = (strip // 2) % 2
    z = strip // 4

    offsets = ((1, 1, 0), (1, 1, 1), (1, 0, 0), (0, 1, 0), (1, 0, 1), (0, 1, 1), (0, 0, 1))

    def plane(n):
        dx, dy, dc = offsets[n]
        return ((x + dx) % 2, (z * 2 + (y + dy) % 2) * 2 + (core + dc) % 2)

    def block_of(dx, dy, dc):
        return ((x + dx) % 2 * 2 + (y + dy) % 2) * 2 + (core + dc + turn(z)) % 2

    def turn(zpos):
        return ((zpos == 1) | (zpos == 2)).astype(jnp.int32)

    me = block_of(0, 0, 0)

    def depth_dev(zpos):
        return (x, (zpos * 2 + y) * 2 + core)

    def depth_swap(zpos):
        return (x, (zpos * 2 + y) * 2 + 1 - core)

    x_dev = (1 - x, (z * 2 + y) * 2 + 1 - core)
    y_dev = (x, (z * 2 + 1 - y) * 2 + 1 - core)
    core_dev = (x, (z * 2 + y) * 2 + 1 - core)
    low_end = z == 0
    high_end = z == depth - 1
    outer = low_end | high_end
    corner_from = (y == 0) & (core == 1)
    corner_to = (y == 0) & (core == 0)

    barrier = pltpu.get_barrier_semaphore()
    for device in (x_dev, y_dev, core_dev):
        pl.semaphore_signal(barrier, inc=1, device_id=device, device_id_type=MESH)

    @pl.when(jnp.logical_not(low_end))
    def _():
        pl.semaphore_signal(barrier, inc=1, device_id=depth_swap(z - 1), device_id_type=MESH)

    @pl.when(jnp.logical_not(high_end))
    def _():
        pl.semaphore_signal(barrier, inc=1, device_id=depth_swap(z + 1), device_id_type=MESH)

    spot = y * 2 + core
    other = (1 - y) * 2 + core
    spot_in = y * 2 + 1 - core
    other_in = (1 - y) * 2 + 1 - core
    loads[0].wait()
    for li in range(layer_dev):
        scr_all[x * layer_dev + li, spot] = scr_ref[li].astype(jnp.float32)

    @pl.when(outer)
    def _():
        pl.semaphore_wait(barrier, 4)

    @pl.when(jnp.logical_not(outer))
    def _():
        pl.semaphore_wait(barrier, 5)

    def remote(src, dst, send, recv, device):
        copy = pltpu.make_async_remote_copy(
            src_ref=src, dst_ref=dst, send_sem=send, recv_sem=recv, device_id=device, device_id_type=MESH
        )
        copy.start()
        return copy

    half = rows_here // HALVES

    def piece(layer, at, h):
        return scr_all.at[layer, at, pl.ds(h * half, half)]

    def share(which, li, h, device):
        n = (which * layer_dev + li) * HALVES + h
        here = piece(x * layer_dev + li, spot, h)
        return remote(here, here, own_send.at[n], own_recv.at[n], device)

    x_copies, y_copies = {}, {}
    for step in range(layer_dev):
        for h in range(HALVES):
            x_copies[step, h] = share(0, step, h, x_dev)
            y_copies[layer_dev - 1 - step, h] = share(1, layer_dev - 1 - step, h, y_dev)
    core_copies = []

    def to_core(here):
        n = len(core_copies)
        core_copies.append(remote(here, here, core_send.at[n], core_recv.at[n], core_dev))

    to_core(scr_all.at[x * layer_dev, spot])
    to_core(scr_all.at[x * layer_dev + 1, spot])

    for load in loads[1:]:
        load.wait()

    layers = [((x + rel) % 2) * layer_dev + li for rel in range(2) for li in range(layer_dev)]
    shrinks = [1.0 - bin_ref[layer].astype(jnp.float32) * bin_step for layer in layers]
    tops = [[row_ref[f, x, layer].astype(jnp.float32) for layer in layers] for f in range(FRAMES)]
    lefts = [[col_ref[f, x, layer].astype(jnp.float32) for layer in layers] for f in range(FRAMES)]

    width = colw.shape[2]
    col_pos = lax.broadcasted_iota(jnp.int32, (columns, width), 0).astype(jnp.float32)
    lane = lax.broadcasted_iota(jnp.int32, (1, width), 1)
    second = lane >= WIDE
    lane = jnp.where(second, lane - WIDE, lane)
    q_of = (
        (lane >= LENSLETS).astype(jnp.int32)
        + (lane >= 2 * LENSLETS).astype(jnp.int32)
        + (lane >= 3 * LENSLETS).astype(jnp.int32)
    )
    pupil_col = ((lane - q_of * LENSLETS) * PIXELS + q_of).astype(jnp.float32)

    def column_weights(n):
        start = pupil_col * shrinks[n] + jnp.where(second, lefts[1][n], lefts[0][n])
        colw[n] = bilinear(col_pos - start).astype(jnp.bfloat16)

    mine = range(layer_dev)
    theirs = range(layer_dev, 2 * layer_dev)
    pair = 2 * rows_here
    stages = (
        (mine, 2 * y, pair),
        (theirs, 2 * y, pair),
        (mine, 2 * (1 - y), pair),
        (theirs, other, rows_here),
        (theirs, 2 * (1 - y) + 1 - core, rows_here),
    )
    begins = [0]
    for members, at, rows in stages:
        begins.append(begins[-1] + len(members) * FRAMES * 2 * rows)

    def row_weights(number):
        members, at, rows = stages[number]
        seg = 2 * rows
        row_pos = lax.broadcasted_iota(jnp.int32, (chunk_rows, seg), 1) % rows + (z * 4 + at) * rows_here
        row_pos = row_pos.astype(jnp.float32)
        row_sub = lax.broadcasted_iota(jnp.int32, (chunk_rows, seg), 0)
        row_base = row_sub // 8 * PIXELS + row_sub % PIXELS
        row_frame = row_sub // PIXELS % FRAMES
        for zpos in range(depth):
            held = jnp.where(z == zpos, core, 1 - core)
            pupil_row = (row_base + ((zpos * 2 + y) * 2 + held) * (arcs * PIXELS)).astype(jnp.float32)
            for i, n in enumerate(members):
                reach = pupil_row * shrinks[n]
                for f in range(FRAMES):
                    weight = jnp.where(row_frame == f, bilinear(row_pos - tops[f][n] - reach), 0.0)
                    lo = begins[number] + (i * FRAMES + f) * seg
                    roww[zpos * chunk_rows : (zpos + 1) * chunk_rows, lo : lo + seg] = weight.astype(jnp.bfloat16)

    def across(number, n):
        members, at, rows = stages[number]
        blocks = rows // rows_here
        source = scr_all[layers[n], pl.ds(at, blocks)].reshape(rows, columns).astype(jnp.bfloat16)
        value = jnp.dot(source, colw[n], preferred_element_type=jnp.float32)
        for f in range(FRAMES):
            one = value[:, f * WIDE : f * WIDE + PUPIL_PIX]
            high = one.astype(jnp.bfloat16)
            low = (one - high.astype(jnp.float32)).astype(jnp.bfloat16)
            lo = begins[number] + ((n - members[0]) * FRAMES + f) * 2 * rows
            rhs[lo : lo + rows, :] = high
            rhs[lo + rows : lo + 2 * rows, :] = low

    def project(number):
        lo, hi = begins[number], begins[number + 1]
        return jnp.dot(roww[:, lo:hi], rhs[lo:hi, :], preferred_element_type=jnp.float32)

    for n in range(2 * layer_dev):
        column_weights(n)
    for number in range(len(stages)):
        row_weights(number)

    passed = {}

    def pass_on(which, h, here, device):
        n = which * HALVES + h
        passed[which, h] = remote(here, here, pass_send.at[n], pass_recv.at[n], device)

    for h in range(HALVES):
        here = piece((1 - x) * layer_dev, spot_in, h)
        x_copies[0, h].wait_recv()
        pass_on(0, h, here, y_dev)
        to_core(here)
        here = piece(x * layer_dev + 1, other_in, h)
        y_copies[1, h].wait_recv()
        pass_on(1, h, here, x_dev)
        to_core(here)
    for copy in core_copies[:2]:
        copy.wait()

    @pl.when(jnp.logical_not(outer))
    def _():
        for zpos in (z - 1, z + 1):
            pl.semaphore_signal(credit.at[0], inc=1, device_id=depth_dev(zpos), device_id_type=MESH)

    for n in mine:
        across(0, n)
    acc[...] = project(0)
    for p in range(PIXELS):
        for q in range(PIXELS):
            for f in range(FRAMES):
                illq[q, f * PIXELS + p : f * PIXELS + p + 1, :] = ill_ref[p * PIXELS + q : p * PIXELS + q + 1, :]
    sat_load.wait()
    for n in range(8):
        some = min(block, actuators - n * block)
        sat[n, 0, :some] = sat_raw[n * block : n * block + some]
    pl.semaphore_wait(credit.at[0], 1)

    @pl.when((z == 1) & corner_from)
    def _():
        pl.semaphore_signal(credit.at[1], inc=1, device_id=depth_dev(z - 1), device_id_type=MESH)

    for h in range(HALVES):
        x_copies[1, h].wait_recv()
        to_core(piece((1 - x) * layer_dev + 1, spot_in, h))
        y_copies[0, h].wait_recv()
        to_core(piece(x * layer_dev, other_in, h))
    for copy in core_copies[2 : 2 + 2 * HALVES]:
        copy.wait()
    across(1, layer_dev)
    across(2, 1)
    for copy in core_copies[2 + 2 * HALVES : 2 + 4 * HALVES]:
        copy.wait()
    across(1, layer_dev + 1)
    across(2, 0)
    for h in range(HALVES):
        passed[0, h].wait_recv()
        to_core(piece((1 - x) * layer_dev, other, h))
        passed[1, h].wait_recv()
        to_core(piece((1 - x) * layer_dev + 1, other, h))
    acc[...] += project(1) + project(2)
    for n in theirs:
        across(3, n)
    acc[...] += project(3)
    for copy in core_copies[2 + 4 * HALVES :]:
        copy.wait()
    for n in theirs:
        across(4, n)
    acc[...] += project(4)
    def pack(zpos):
        value = acc[pl.ds(pl.multiple_of(zpos * chunk_rows, chunk_rows), chunk_rows), :]
        for a in range(arcs):
            lines = value[a * 8 : (a + 1) * 8]
            for t in range(full):
                at = tile_of(arcs, a, t) * 8
                part[zpos, at : at + 8, :] = lines[:, t * 128 : (t + 1) * 128]
            at = tile_of(arcs, a, full) * 8
            lane0 = a % 2 * rest
            part[zpos, at : at + 8, lane0 : lane0 + rest] = lines[:, full * 128 :]
        if arcs % 2:
            at = tile_of(arcs, arcs - 1, full) * 8
            part[zpos, at : at + 8, rest:] = jnp.zeros((8, 128 - rest), jnp.float32)

    edge = tile_of(arcs, 1, full) + 1
    tiles = packed_tiles(arcs)
    pieces = [pl.ds(edge * 8, (tiles - edge) * 8), pl.ds(0, edge * 8)]
    count = len(pieces)
    ahead = jnp.where(z < depth // 2, 1, -1)

    def z_copy(send, slot_at, i, zpos):
        return pltpu.make_async_remote_copy(
            src_ref=part.at[zpos, pieces[i]],
            dst_ref=z_in.at[slot_at, pieces[i]],
            send_sem=z_send.at[send * count + i],
            recv_sem=z_recv.at[slot_at * count + i],
            device_id=depth_swap(zpos),
            device_id_type=MESH,
        )

    far_copy = pltpu.make_async_remote_copy(
        src_ref=part.at[depth - 1, pieces[1]],
        dst_ref=far_in,
        send_sem=far_send,
        recv_sem=far_recv,
        device_id=depth_swap(depth - 1),
        device_id_type=MESH,
    )
    sends = [(z + 2 * ahead, 0), (z + ahead, jnp.where(outer, 2, 1))]
    for n, (zpos, slot_at) in enumerate(sends):
        pack(zpos)
        for i in range(count):
            z_copy(n, slot_at, i, zpos).start()

    @pl.when(jnp.logical_not(outer))
    def _():
        pack(z - ahead)
        for i in range(count):
            z_copy(2, 1, i, z - ahead).start()

    @pl.when(low_end & corner_from)
    def _():
        pack(depth - 1)
        pl.semaphore_wait(credit.at[1], 1)
        far_copy.start()

    pack(z)
    for i, rows in enumerate(pieces):

        @pl.when(jnp.logical_not(outer))
        def _():
            z_copy(0, 2, i, z - ahead).wait_recv()
            part[z, rows] = part[z, rows] + z_in[2, rows]

        z_copy(0, 1, i, z + ahead).wait_recv()
        z_copy(0, 0, i, z + 2 * ahead).wait_recv()
        phase_sc[rows] = part[z, rows] + z_in[0, rows] + z_in[1, rows]

    @pl.when(high_end & corner_to)
    def _():
        far_copy.wait_recv()
        phase_sc[pieces[1]] = phase_sc[pieces[1]] + far_in[...]

    for a in range(arcs):
        for q in range(PIXELS):
            lo = q * LENSLETS
            while lo < (q + 1) * LENSLETS:
                t = lo // 128
                hi = min((q + 1) * LENSLETS, (t + 1) * 128)
                at = tile_of(arcs, a, t) * 8
                lane0 = lo - t * 128 + (a % 2 * rest if t == full else 0)
                to = a * LENSLETS + lo - q * LENSLETS
                phiq[q, :, to : to + hi - lo] = phase_sc[at : at + 8, lane0 : lane0 + hi - lo]
                lo = hi

    cosines, sines = [], []
    flux = None
    for q in range(PIXELS):
        amp = illq[q]
        phi = phiq[q]
        cosines.append(amp * jnp.cos(phi))
        sines.append(amp * jnp.sin(phi))
        flux = amp * amp if flux is None else flux + amp * amp
    tip = -float(PIXELS) * flux
    tilt = tip
    pix_row = lax.broadcasted_iota(jnp.int32, flux.shape, 0) % PIXELS
    for d in range(1, PIXELS):
        gain = pair_gain(d)
        even = -2.0 * PIXELS * (-1.0) ** d
        term = None
        for q in range(d, PIXELS):
            ch, sh, cl, sl = cosines[q], sines[q], cosines[q - d], sines[q - d]
            new = gain * (sh * cl - ch * sl) + even * (ch * cl + sh * sl)
            term = new if term is None else term + new
        tilt = tilt + term
        term = None
        for q in range(PIXELS):
            ch, sh = cosines[q], sines[q]
            cl, sl = pltpu.roll(ch, d, 0), pltpu.roll(sh, d, 0)
            new = gain * (sh * cl - ch * sl) + even * (ch * cl + sh * sl)
            term = new if term is None else term + new
        tip = tip + jnp.where(pix_row >= d, term, 0.0)
    for f in range(FRAMES):
        rows = slice(f * PIXELS, (f + 1) * PIXELS)
        total = jnp.sum(flux[rows], axis=0, keepdims=True) * (2.0 * PIXELS)
        for c, value in enumerate((tip, tilt)):
            slope = jnp.sum(value[rows], axis=0, keepdims=True) / total
            slopes_out[f, c : c + 1, :] = slope
            slope_sc[c, f : f + 1, :] = slope

    rec_copy.wait()
    rounded = [slope_sc[c].astype(jnp.bfloat16) for c in range(2)]
    tail = actuators - 7 * block
    whole = tail // 128 * 128

    def update(to):
        def some(cols):
            value = jnp.dot(rounded[0], rec[0, :, cols], preferred_element_type=jnp.float32)
            return value + jnp.dot(rounded[1], rec[1, :, cols], preferred_element_type=jnp.float32)

        @pl.when(to < 7)
        def _():
            upd[to] = some(pl.ds(pl.multiple_of(to * block, 128), block))

        @pl.when(to == 7)
        def _():
            upd[7, :, whole:] = jnp.zeros((FRAMES, block - whole), jnp.float32)
            upd[7, :, :tail] = some(slice(7 * block, actuators))

    def b_dev(zpos):
        return (x, (zpos * 2 + y) * 2 + (core + turn(z) + turn(zpos)) % 2)

    copies = []
    for n in range(7):
        to = block_of(*offsets[n])
        update(to)
        copies.append(remote(upd.at[to], gathered.at[n], a_send.at[n], a_recv.at[n], plane(n)))
    update(me)
    for copy in copies:
        copy.wait_recv()
    drain = copies
    total = upd[me]
    for n in range(7):
        total = total + gathered[n]
    zsum[z] = total
    copies = []
    for k in range(1, depth):
        copies.append(
            remote(zsum.at[z], zsum.at[z], b_send.at[k - 1], b_recv.at[k - 1], b_dev((z + k) % depth))
        )
    for copy in copies:
        copy.wait_recv()
    drain = drain + copies
    total = zsum[0]
    for k in range(1, depth):
        total = total + zsum[k]
    limits = sat[me].astype(jnp.float32) * code_step
    first_cmd = jnp.clip(loop_gain * total[:1], -limits, limits)
    second_cmd = jnp.clip(first_cmd + loop_gain * total[1:], -limits, limits)
    gathered[0, :1] = first_cmd
    gathered[0, 1:] = second_cmd
    own_cols = pl.ds(pl.multiple_of(me * block, 128), block)
    upd_out[:, own_cols] = gathered[0]
    copies = []
    for n in range(7):
        copies.append(
            remote(upd_out.at[:, own_cols], upd_out.at[:, own_cols], c_send.at[n], c_recv.at[n], plane(n))
        )
    for copy in list(x_copies.values()) + list(y_copies.values()) + list(passed.values()):
        copy.wait_send()
    for n, (zpos, slot_at) in enumerate(sends):
        for i in range(count):
            z_copy(n, slot_at, i, zpos).wait_send()

    @pl.when(jnp.logical_not(outer))
    def _():
        for i in range(count):
            z_copy(2, 1, i, z - ahead).wait_send()

    @pl.when(low_end & corner_from)
    def _():
        far_copy.wait_send()

    for copy in copies:
        copy.wait()
    for copy in drain:
        copy.wait_send()


def fused_shards(screens, row_offset, col_offset, layer_bin, illumination, reconstructor, sat_code):
    layer_dev, rows_here, columns = screens.shape
    count_here = illumination.shape[1]
    actuators = reconstructor.shape[2]
    depth = PLANES
    arcs = count_here // LENSLETS
    chunk = (packed_tiles(arcs) * 8, 128)
    edge = ((tile_of(arcs, 1, PUPIL_PIX // 128) + 1) * 8, 128)
    rows = padded_rows(arcs)
    block = -(-actuators // (8 * 128)) * 128
    contraction = FRAMES * 2 * 2 * layer_dev * 4 * rows_here
    width = (FRAMES - 1) * WIDE + PUPIL_PIX
    dma = pltpu.SemaphoreType.DMA
    spots = (FRAMES, GUIDE_STARS, row_offset.shape[1])
    vmem = pl.BlockSpec(memory_space=pltpu.VMEM)

    def in_hbm(value):
        return pltpu.with_memory_space_constraint(value, pltpu.HBM)

    slopes, updates = pl.pallas_call(
        functools.partial(fused_kernel, block),
        out_shape=(
            jax.ShapeDtypeStruct((FRAMES, 2, count_here), jnp.float32),
            jax.ShapeDtypeStruct((FRAMES, 8 * block), jnp.float32),
        ),
        in_specs=[pl.BlockSpec(memory_space=pltpu.HBM)] * 7,
        out_specs=(vmem, vmem),
        scratch_shapes=[
            pltpu.VMEM(screens.shape, jnp.bfloat16),
            pltpu.SMEM(spots, jnp.int32),
            pltpu.SMEM(spots, jnp.int32),
            pltpu.SMEM(layer_bin.shape, jnp.int32),
            pltpu.VMEM(illumination.shape, jnp.float32),
            pltpu.VMEM((2 * layer_dev, 4, rows_here, columns), jnp.float32),
            pltpu.VMEM((2 * layer_dev, columns, width), jnp.bfloat16),
            pltpu.VMEM((depth * rows, contraction), jnp.bfloat16),
            pltpu.VMEM((contraction, PUPIL_PIX), jnp.bfloat16),
            pltpu.VMEM((depth * rows, PUPIL_PIX), jnp.float32),
            pltpu.VMEM((depth,) + chunk, jnp.float32),
            pltpu.VMEM((3,) + chunk, jnp.float32),
            pltpu.VMEM(edge, jnp.float32),
            pltpu.VMEM(chunk, jnp.float32),
            pltpu.VMEM((PIXELS, FRAMES * PIXELS, count_here), jnp.float32),
            pltpu.VMEM((PIXELS, FRAMES * PIXELS, count_here), jnp.float32),
            pltpu.VMEM((2, FRAMES, count_here), jnp.float32),
            pltpu.VMEM(reconstructor.shape, jnp.bfloat16),
            pltpu.VMEM((8, FRAMES, block), jnp.float32),
            pltpu.VMEM((7, FRAMES, block), jnp.float32),
            pltpu.VMEM((depth, FRAMES, block), jnp.float32),
            pltpu.VMEM((actuators,), jnp.int32),
            pltpu.VMEM((8, 1, block), jnp.int32),
            dma((5,)), dma, dma,
            dma((2 * layer_dev * HALVES,)), dma((2 * layer_dev * HALVES,)),
            dma((2 * HALVES,)), dma((2 * HALVES,)),
            dma((2 + 6 * HALVES,)), dma((2 + 6 * HALVES,)),
            dma((6,)), dma((6,)), dma, dma,
            pltpu.SemaphoreType.REGULAR((2,)),
            dma((7,)), dma((7,)),
            dma((depth - 1,)), dma((depth - 1,)),
            dma((7,)), dma((7,)),
        ],
        compiler_params=pltpu.CompilerParams(collective_id=0, has_side_effects=True, vmem_limit_bytes=44 * 2**20),
        name="fused",
    )(
        in_hbm(screens),
        in_hbm(row_offset.transpose(0, 2, 1)),
        in_hbm(col_offset.transpose(0, 2, 1)),
        in_hbm(layer_bin),
        in_hbm(illumination),
        in_hbm(reconstructor),
        in_hbm(sat_code),
    )
    return slopes, updates[:, :actuators]


def step(screens, row_offset, col_offset, layer_bin, illumination, reconstructor, sat_code):
    strips = lax.axis_size("strip")
    fused = (
        lax.axis_size("alt") == 2 == GUIDE_STARS
        and strips == 4 * PLANES
        and screens.shape[0] == 2
        and LENSLETS % strips == 0
        and LENSLETS // strips > 2
        and screens.shape[1] % 16 == 0
        and far_pattern(strips * screens.shape[1], LENSLETS // strips)
    )
    chosen = fused_shards if fused else shards
    return chosen(screens, row_offset, col_offset, layer_bin, illumination, reconstructor, sat_code)


def solution(mesh):
    placed = (
        P("alt", "strip", None),
        P(),
        P(),
        P(),
        P(None, ("alt", "strip")),
        P(None, ("alt", "strip"), None),
        P(),
    )
    return jax.shard_map(
        step,
        mesh=mesh,
        in_specs=placed,
        out_specs=(P(None, None, ("alt", "strip")), P()),
        check_vma=False,
    )
```

```python
import functools
import math

import jax
import jax.numpy as jnp
from jax import lax
from jax.experimental import pallas as pl
from jax.experimental.pallas import tpu as pltpu
from jax.sharding import PartitionSpec as P

LENSLETS = 80
PIXELS = 4
GUIDE_STARS = 2
FRAMES = 2
ACTUATORS = 6000
PUPIL_PIX = 320
WINDOW = 384
SUBAPS_ALL = 12800


highest = lax.Precision.HIGHEST
loop_gain = 0.5
code_step = 0.125
bin_step = 0.03125


def bilinear(offsets):
    return jnp.maximum(0.0, 1.0 - jnp.abs(offsets))


def dft_tables():
    padded = 2 * PIXELS
    freq_index = jnp.arange(padded * padded, dtype=jnp.int32)
    freq_row = freq_index // padded
    freq_col = freq_index % padded
    pix_index = jnp.arange(PIXELS * PIXELS, dtype=jnp.int32)
    pix_row = pix_index // PIXELS
    pix_col = pix_index % PIXELS
    turn_count = (
        freq_row[:, None] * pix_row[None, :] + freq_col[:, None] * pix_col[None, :]
    ) % padded
    angles = turn_count.astype(jnp.float32) * (2.0 * math.pi / padded)
    coord_row = ((freq_row + PIXELS) % padded - PIXELS).astype(jnp.float32)
    coord_col = ((freq_col + PIXELS) % padded - PIXELS).astype(jnp.float32)
    return (jnp.cos(angles), jnp.sin(angles), coord_row, coord_col)


def centroids(pupil_phase, illumination, tables):
    cosine, sine_table, coord_row, coord_col = tables
    field_re = illumination * jnp.cos(pupil_phase)
    field_im = illumination * jnp.sin(pupil_phase)
    real_part = jnp.dot(cosine, field_re, precision=highest) + jnp.dot(
        sine_table, field_im, precision=highest
    )
    imag_part = jnp.dot(cosine, field_im, precision=highest) - jnp.dot(
        sine_table, field_re, precision=highest
    )
    intensity = real_part * real_part + imag_part * imag_part
    flux_sum = jnp.sum(intensity, axis=0)
    slope_row = jnp.sum(intensity * coord_row[:, None], axis=0) / flux_sum
    slope_col = jnp.sum(intensity * coord_col[:, None], axis=0) / flux_sum
    return jnp.stack([slope_row, slope_col])


def shards(screens, row_offset, col_offset, layer_bin, illumination, reconstructor, sat_code):
    layer_dev = screens.shape[0]
    rows_here = screens.shape[1]
    count_here = illumination.shape[1]
    group_pos = lax.axis_index("alt")
    strip_pos = lax.axis_index("strip")
    row_global = strip_pos * rows_here + jnp.arange(rows_here, dtype=jnp.int32)
    pupil_idx = jnp.arange(PUPIL_PIX, dtype=jnp.float32)
    window_idx = jnp.arange(WINDOW, dtype=jnp.float32)
    widened_layers = [
        jnp.pad(screens[layer_no], ((0, 0), (0, WINDOW))) for layer_no in range(layer_dev)
    ]
    frame_terms = []
    for frame_no in range(FRAMES):
        running = jnp.zeros((PIXELS, PIXELS, GUIDE_STARS, LENSLETS, LENSLETS), jnp.float32)
        for layer_no in range(layer_dev):
            layer_pos = group_pos * layer_dev + layer_no
            tops = lax.dynamic_index_in_dim(row_offset[frame_no], layer_pos, 0, keepdims=False)
            lefts = lax.dynamic_index_in_dim(col_offset[frame_no], layer_pos, 0, keepdims=False)
            bin_value = lax.dynamic_index_in_dim(layer_bin, layer_pos, 0, keepdims=False)
            shrink = 1.0 - bin_value.astype(jnp.float32) * bin_step
            col_weights = bilinear(window_idx[None, :] - pupil_idx[:, None] * shrink)
            widened = widened_layers[layer_no]

            def cut_columns(left_col):
                return lax.dynamic_slice_in_dim(widened, left_col, WINDOW, 1)

            strips = jax.vmap(cut_columns)(lefts).astype(jnp.float32)
            across = jnp.einsum("drc,jc->drj", strips, col_weights, precision=highest)
            offsets = (row_global[None, :] - tops[:, None]).astype(jnp.float32)
            row_weights = bilinear(offsets[:, None, :] - pupil_idx[None, :, None] * shrink)
            running = running + jnp.einsum(
                "dapr,drbq->pqdab",
                row_weights.reshape(GUIDE_STARS, LENSLETS, PIXELS, rows_here),
                across.reshape(GUIDE_STARS, rows_here, LENSLETS, PIXELS),
                precision=highest,
            )
        frame_terms.append(running.reshape(PIXELS * PIXELS, SUBAPS_ALL))
    phase_terms = jnp.concatenate(frame_terms, axis=0)
    partly = lax.psum_scatter(phase_terms, "alt", scatter_dimension=1, tiled=True)
    owned = lax.psum_scatter(partly, "strip", scatter_dimension=1, tiled=True)
    pupil_phase = owned.reshape(FRAMES, PIXELS * PIXELS, count_here)
    tables = dft_tables()
    slopes = jnp.stack(
        [centroids(pupil_phase[frame_no], illumination, tables) for frame_no in range(FRAMES)]
    )
    rounded = slopes.astype(jnp.bfloat16).reshape(FRAMES, 2 * count_here)
    partial_value = jnp.dot(
        rounded,
        reconstructor.reshape(2 * count_here, ACTUATORS),
        preferred_element_type=jnp.float32,
    )
    updates = lax.psum(partial_value, ("alt", "strip"))
    limits = sat_code.astype(jnp.float32) * code_step
    first_cmd = jnp.clip(loop_gain * updates[0], -limits, limits)
    second_cmd = jnp.clip(first_cmd + loop_gain * updates[1], -limits, limits)
    return (slopes, jnp.stack([first_cmd, second_cmd]))


MESH = pl.DeviceIdType.MESH
HALVES = 1
PLANES = 4
WIDE = -(-PUPIL_PIX // 128) * 128


def pair_gain(distance):
    turn = 2.0 * math.pi / (2 * PIXELS)
    return 4.0 * sum(k * math.sin(turn * k * distance) for k in range(1, PIXELS))


def padded_rows(arcs):
    return -(-arcs * FRAMES * PIXELS // 16) * 16


def tile_of(arcs, arc, part):
    full = PUPIL_PIX // 128
    pair = arc // 2 * (2 * full + 1)
    if part < full:
        return pair + arc % 2 * full + part
    return pair + (2 * full if arc // 2 * 2 + 1 < arcs else full)


def packed_tiles(arcs):
    return tile_of(arcs, arcs - 1, PUPIL_PIX // 128) + 1


def reaches(total, rows, first, last):
    for layer_bin in range(16):
        shrink = 1.0 - layer_bin * bin_step
        top = math.floor(total - 1 - (PUPIL_PIX - 1) * shrink)
        if top + last * shrink > rows[0] - 1 and first * shrink < rows[1] + 1:
            return True
    return False


def far_pattern(total, arcs):
    plane_rows = total // PLANES
    strip_rows = arcs * PIXELS
    for strip in range(4):
        first = strip * strip_rows
        if reaches(total, (total - plane_rows, total - 1), first, first + strip_rows - 1):
            return False
        first += (PLANES - 1) * 4 * strip_rows
        low = first + 2 * PIXELS if strip == 0 else first
        if reaches(total, (0, plane_rows - 1), low, first + strip_rows - 1):
            return False
    return True


def fused_kernel(
    block,
    scr_hbm,
    row_hbm,
    col_hbm,
    bin_hbm,
    ill_hbm,
    rec_hbm,
    sat_hbm,
    slopes_out,
    upd_out,
    scr_ref,
    row_ref,
    col_ref,
    bin_ref,
    ill_ref,
    scr_all,
    colw,
    roww,
    rhs,
    acc,
    part,
    z_in,
    far_in,
    phase_sc,
    phiq,
    illq,
    slope_sc,
    rec,
    upd,
    gathered,
    zsum,
    sat_raw,
    sat,
    in_sem,
    rec_sem,
    sat_sem,
    own_send,
    own_recv,
    pass_send,
    pass_recv,
    core_send,
    core_recv,
    z_send,
    z_recv,
    far_send,
    far_recv,
    credit,
    a_send,
    a_recv,
    b_send,
    b_recv,
    c_send,
    c_recv,
):
    layer_dev, rows_here, columns = scr_ref.shape
    count_here = ill_ref.shape[1]
    arcs = count_here // LENSLETS
    chunk_rows = padded_rows(arcs)
    depth = PLANES
    full = PUPIL_PIX // 128
    rest = PUPIL_PIX - full * 128
    actuators = rec_hbm.shape[2]

    loads = [
        pltpu.make_async_copy(src, dst, in_sem.at[n])
        for n, (src, dst) in enumerate(
            (
                (scr_hbm, scr_ref),
                (row_hbm, row_ref),
                (col_hbm, col_ref),
                (bin_hbm, bin_ref),
                (ill_hbm, ill_ref),
            )
        )
    ]
    for load in loads:
        load.start()
    rec_copy = pltpu.make_async_copy(rec_hbm, rec, rec_sem)
    rec_copy.start()
    sat_load = pltpu.make_async_copy(sat_hbm, sat_raw, sat_sem)
    sat_load.start()

    x = lax.axis_index("alt")
    strip = lax.axis_index("strip")
    core = strip % 2
    y = (strip // 2) % 2
    z = strip // 4

    offsets = ((1, 1, 0), (1, 1, 1), (1, 0, 0), (0, 1, 0), (1, 0, 1), (0, 1, 1), (0, 0, 1))

    def plane(n):
        dx, dy, dc = offsets[n]
        return ((x + dx) % 2, (z * 2 + (y + dy) % 2) * 2 + (core + dc) % 2)

    def block_of(dx, dy, dc):
        return ((x + dx) % 2 * 2 + (y + dy) % 2) * 2 + (core + dc + turn(z)) % 2

    def turn(zpos):
        return ((zpos == 1) | (zpos == 2)).astype(jnp.int32)

    me = block_of(0, 0, 0)

    def depth_dev(zpos):
        return (x, (zpos * 2 + y) * 2 + core)

    def depth_swap(zpos):
        return (x, (zpos * 2 + y) * 2 + 1 - core)

    x_dev = (1 - x, (z * 2 + y) * 2 + 1 - core)
    y_dev = (x, (z * 2 + 1 - y) * 2 + 1 - core)
    core_dev = (x, (z * 2 + y) * 2 + 1 - core)
    low_end = z == 0
    high_end = z == depth - 1
    outer = low_end | high_end
    corner_from = (y == 0) & (core == 1)
    corner_to = (y == 0) & (core == 0)

    barrier = pltpu.get_barrier_semaphore()
    for device in (x_dev, y_dev, core_dev):
        pl.semaphore_signal(barrier, inc=1, device_id=device, device_id_type=MESH)

    @pl.when(jnp.logical_not(low_end))
    def _():
        pl.semaphore_signal(barrier, inc=1, device_id=depth_swap(z - 1), device_id_type=MESH)

    @pl.when(jnp.logical_not(high_end))
    def _():
        pl.semaphore_signal(barrier, inc=1, device_id=depth_swap(z + 1), device_id_type=MESH)

    spot = y * 2 + core
    other = (1 - y) * 2 + core
    spot_in = y * 2 + 1 - core
    other_in = (1 - y) * 2 + 1 - core
    loads[0].wait()
    for li in range(layer_dev):
        scr_all[x * layer_dev + li, spot] = scr_ref[li].astype(jnp.float32)

    @pl.when(outer)
    def _():
        pl.semaphore_wait(barrier, 4)

    @pl.when(jnp.logical_not(outer))
    def _():
        pl.semaphore_wait(barrier, 5)

    def remote(src, dst, send, recv, device):
        copy = pltpu.make_async_remote_copy(
            src_ref=src, dst_ref=dst, send_sem=send, recv_sem=recv, device_id=device, device_id_type=MESH
        )
        copy.start()
        return copy

    half = rows_here // HALVES

    def piece(layer, at, h):
        return scr_all.at[layer, at, pl.ds(h * half, half)]

    def share(which, li, h, device):
        n = (which * layer_dev + li) * HALVES + h
        here = piece(x * layer_dev + li, spot, h)
        return remote(here, here, own_send.at[n], own_recv.at[n], device)

    x_copies, y_copies = {}, {}
    for step in range(layer_dev):
        for h in range(HALVES):
            x_copies[step, h] = share(0, step, h, x_dev)
            y_copies[layer_dev - 1 - step, h] = share(1, layer_dev - 1 - step, h, y_dev)
    core_copies = []

    def to_core(here):
        n = len(core_copies)
        core_copies.append(remote(here, here, core_send.at[n], core_recv.at[n], core_dev))

    to_core(scr_all.at[x * layer_dev, spot])
    to_core(scr_all.at[x * layer_dev + 1, spot])

    for load in loads[1:]:
        load.wait()

    layers = [((x + rel) % 2) * layer_dev + li for rel in range(2) for li in range(layer_dev)]
    shrinks = [1.0 - bin_ref[layer].astype(jnp.float32) * bin_step for layer in layers]
    tops = [[row_ref[f, x, layer].astype(jnp.float32) for layer in layers] for f in range(FRAMES)]
    lefts = [[col_ref[f, x, layer].astype(jnp.float32) for layer in layers] for f in range(FRAMES)]

    width = colw.shape[2]
    col_pos = lax.broadcasted_iota(jnp.int32, (columns, width), 0).astype(jnp.float32)
    lane = lax.broadcasted_iota(jnp.int32, (1, width), 1)
    second = lane >= WIDE
    lane = jnp.where(second, lane - WIDE, lane)
    q_of = (
        (lane >= LENSLETS).astype(jnp.int32)
        + (lane >= 2 * LENSLETS).astype(jnp.int32)
        + (lane >= 3 * LENSLETS).astype(jnp.int32)
    )
    pupil_col = ((lane - q_of * LENSLETS) * PIXELS + q_of).astype(jnp.float32)

    def column_weights(n):
        start = pupil_col * shrinks[n] + jnp.where(second, lefts[1][n], lefts[0][n])
        colw[n] = bilinear(col_pos - start).astype(jnp.bfloat16)

    mine = range(layer_dev)
    theirs = range(layer_dev, 2 * layer_dev)
    pair = 2 * rows_here
    stages = (
        (mine, 2 * y, pair),
        (theirs, 2 * y, pair),
        (mine, 2 * (1 - y), pair),
        (theirs, other, rows_here),
        (theirs, 2 * (1 - y) + 1 - core, rows_here),
    )
    begins = [0]
    for members, at, rows in stages:
        begins.append(begins[-1] + len(members) * FRAMES * 2 * rows)

    def row_weights(number):
        members, at, rows = stages[number]
        seg = 2 * rows
        row_pos = lax.broadcasted_iota(jnp.int32, (chunk_rows, seg), 1) % rows + (z * 4 + at) * rows_here
        row_pos = row_pos.astype(jnp.float32)
        row_sub = lax.broadcasted_iota(jnp.int32, (chunk_rows, seg), 0)
        row_base = row_sub // 8 * PIXELS + row_sub % PIXELS
        row_frame = row_sub // PIXELS % FRAMES
        for zpos in range(depth):
            held = jnp.where(z == zpos, core, 1 - core)
            pupil_row = (row_base + ((zpos * 2 + y) * 2 + held) * (arcs * PIXELS)).astype(jnp.float32)
            for i, n in enumerate(members):
                reach = pupil_row * shrinks[n]
                for f in range(FRAMES):
                    weight = jnp.where(row_frame == f, bilinear(row_pos - tops[f][n] - reach), 0.0)
                    lo = begins[number] + (i * FRAMES + f) * seg
                    roww[zpos * chunk_rows : (zpos + 1) * chunk_rows, lo : lo + seg] = weight.astype(jnp.bfloat16)

    def across(number, n):
        members, at, rows = stages[number]
        blocks = rows // rows_here
        source = scr_all[layers[n], pl.ds(at, blocks)].reshape(rows, columns).astype(jnp.bfloat16)
        value = jnp.dot(source, colw[n], preferred_element_type=jnp.float32)
        for f in range(FRAMES):
            one = value[:, f * WIDE : f * WIDE + PUPIL_PIX]
            high = one.astype(jnp.bfloat16)
            low = (one - high.astype(jnp.float32)).astype(jnp.bfloat16)
            lo = begins[number] + ((n - members[0]) * FRAMES + f) * 2 * rows
            rhs[lo : lo + rows, :] = high
            rhs[lo + rows : lo + 2 * rows, :] = low

    def project(number):
        lo, hi = begins[number], begins[number + 1]
        return jnp.dot(roww[:, lo:hi], rhs[lo:hi, :], preferred_element_type=jnp.float32)

    for n in range(2 * layer_dev):
        column_weights(n)
    for number in range(len(stages)):
        row_weights(number)

    passed = {}

    def pass_on(which, h, here, device):
        n = which * HALVES + h
        passed[which, h] = remote(here, here, pass_send.at[n], pass_recv.at[n], device)

    for h in range(HALVES):
        here = piece((1 - x) * layer_dev, spot_in, h)
        x_copies[0, h].wait_recv()
        pass_on(0, h, here, y_dev)
        to_core(here)
        here = piece(x * layer_dev + 1, other_in, h)
        y_copies[1, h].wait_recv()
        pass_on(1, h, here, x_dev)
        to_core(here)
    for copy in core_copies[:2]:
        copy.wait()

    @pl.when(jnp.logical_not(outer))
    def _():
        for zpos in (z - 1, z + 1):
            pl.semaphore_signal(credit.at[0], inc=1, device_id=depth_dev(zpos), device_id_type=MESH)

    for n in mine:
        across(0, n)
    acc[...] = project(0)
    for p in range(PIXELS):
        for q in range(PIXELS):
            for f in range(FRAMES):
                illq[q, f * PIXELS + p : f * PIXELS + p + 1, :] = ill_ref[p * PIXELS + q : p * PIXELS + q + 1, :]
    sat_load.wait()
    for n in range(8):
        some = min(block, actuators - n * block)
        sat[n, 0, :some] = sat_raw[n * block : n * block + some]
    pl.semaphore_wait(credit.at[0], 1)

    @pl.when((z == 1) & corner_from)
    def _():
        pl.semaphore_signal(credit.at[1], inc=1, device_id=depth_dev(z - 1), device_id_type=MESH)

    for h in range(HALVES):
        x_copies[1, h].wait_recv()
        to_core(piece((1 - x) * layer_dev + 1, spot_in, h))
        y_copies[0, h].wait_recv()
        to_core(piece(x * layer_dev, other_in, h))
    for copy in core_copies[2 : 2 + 2 * HALVES]:
        copy.wait()
    across(1, layer_dev)
    across(2, 1)
    for copy in core_copies[2 + 2 * HALVES : 2 + 4 * HALVES]:
        copy.wait()
    across(1, layer_dev + 1)
    across(2, 0)
    for h in range(HALVES):
        passed[0, h].wait_recv()
        to_core(piece((1 - x) * layer_dev, other, h))
        passed[1, h].wait_recv()
        to_core(piece((1 - x) * layer_dev + 1, other, h))
    acc[...] += project(1) + project(2)
    for n in theirs:
        across(3, n)
    acc[...] += project(3)
    for copy in core_copies[2 + 4 * HALVES :]:
        copy.wait()
    for n in theirs:
        across(4, n)
    acc[...] += project(4)
    def pack(zpos):
        value = acc[pl.ds(pl.multiple_of(zpos * chunk_rows, chunk_rows), chunk_rows), :]
        for a in range(arcs):
            lines = value[a * 8 : (a + 1) * 8]
            for t in range(full):
                at = tile_of(arcs, a, t) * 8
                part[zpos, at : at + 8, :] = lines[:, t * 128 : (t + 1) * 128]
            at = tile_of(arcs, a, full) * 8
            lane0 = a % 2 * rest
            part[zpos, at : at + 8, lane0 : lane0 + rest] = lines[:, full * 128 :]
        if arcs % 2:
            at = tile_of(arcs, arcs - 1, full) * 8
            part[zpos, at : at + 8, rest:] = jnp.zeros((8, 128 - rest), jnp.float32)

    edge = tile_of(arcs, 1, full) + 1
    tiles = packed_tiles(arcs)
    pieces = [pl.ds(edge * 8, (tiles - edge) * 8), pl.ds(0, edge * 8)]
    count = len(pieces)
    ahead = jnp.where(z < depth // 2, 1, -1)

    def z_copy(send, slot_at, i, zpos):
        return pltpu.make_async_remote_copy(
            src_ref=part.at[zpos, pieces[i]],
            dst_ref=z_in.at[slot_at, pieces[i]],
            send_sem=z_send.at[send * count + i],
            recv_sem=z_recv.at[slot_at * count + i],
            device_id=depth_swap(zpos),
            device_id_type=MESH,
        )

    far_copy = pltpu.make_async_remote_copy(
        src_ref=part.at[depth - 1, pieces[1]],
        dst_ref=far_in,
        send_sem=far_send,
        recv_sem=far_recv,
        device_id=depth_swap(depth - 1),
        device_id_type=MESH,
    )
    sends = [(z + 2 * ahead, 0), (z + ahead, jnp.where(outer, 2, 1))]
    @pl.when(jnp.logical_not(outer))
    def _():
        pack(z - ahead)
        for i in range(count):
            z_copy(2, 1, i, z - ahead).start()

    pack(sends[0][0])
    for i in range(count):
        z_copy(0, sends[0][1], i, sends[0][0]).start()

    pack(sends[1][0])
    for i in range(count):
        z_copy(1, sends[1][1], i, sends[1][0]).start()

    @pl.when(low_end & corner_from)
    def _():
        pack(depth - 1)
        pl.semaphore_wait(credit.at[1], 1)
        far_copy.start()

    pack(z)
    for i, rows in enumerate(pieces):

        @pl.when(jnp.logical_not(outer))
        def _():
            z_copy(0, 2, i, z - ahead).wait_recv()
            part[z, rows] = part[z, rows] + z_in[2, rows]

        z_copy(0, 1, i, z + ahead).wait_recv()
        z_copy(0, 0, i, z + 2 * ahead).wait_recv()
        phase_sc[rows] = part[z, rows] + z_in[0, rows] + z_in[1, rows]

    @pl.when(high_end & corner_to)
    def _():
        far_copy.wait_recv()
        phase_sc[pieces[1]] = phase_sc[pieces[1]] + far_in[...]

    for a in range(arcs):
        for q in range(PIXELS):
            lo = q * LENSLETS
            while lo < (q + 1) * LENSLETS:
                t = lo // 128
                hi = min((q + 1) * LENSLETS, (t + 1) * 128)
                at = tile_of(arcs, a, t) * 8
                lane0 = lo - t * 128 + (a % 2 * rest if t == full else 0)
                to = a * LENSLETS + lo - q * LENSLETS
                phiq[q, :, to : to + hi - lo] = phase_sc[at : at + 8, lane0 : lane0 + hi - lo]
                lo = hi

    cosines, sines = [], []
    flux = None
    for q in range(PIXELS):
        amp = illq[q]
        phi = phiq[q]
        cosines.append(amp * jnp.cos(phi))
        sines.append(amp * jnp.sin(phi))
        flux = amp * amp if flux is None else flux + amp * amp
    tip = -float(PIXELS) * flux
    tilt = tip
    pix_row = lax.broadcasted_iota(jnp.int32, flux.shape, 0) % PIXELS
    for d in range(1, PIXELS):
        gain = pair_gain(d)
        even = -2.0 * PIXELS * (-1.0) ** d
        term = None
        for q in range(d, PIXELS):
            ch, sh, cl, sl = cosines[q], sines[q], cosines[q - d], sines[q - d]
            new = gain * (sh * cl - ch * sl) + even * (ch * cl + sh * sl)
            term = new if term is None else term + new
        tilt = tilt + term
        term = None
        for q in range(PIXELS):
            ch, sh = cosines[q], sines[q]
            cl, sl = pltpu.roll(ch, d, 0), pltpu.roll(sh, d, 0)
            new = gain * (sh * cl - ch * sl) + even * (ch * cl + sh * sl)
            term = new if term is None else term + new
        tip = tip + jnp.where(pix_row >= d, term, 0.0)
    for f in range(FRAMES):
        rows = slice(f * PIXELS, (f + 1) * PIXELS)
        total = jnp.sum(flux[rows], axis=0, keepdims=True) * (2.0 * PIXELS)
        for c, value in enumerate((tip, tilt)):
            slope = jnp.sum(value[rows], axis=0, keepdims=True) / total
            slopes_out[f, c : c + 1, :] = slope
            slope_sc[c, f : f + 1, :] = slope

    rec_copy.wait()
    rounded = [slope_sc[c].astype(jnp.bfloat16) for c in range(2)]
    tail = actuators - 7 * block
    whole = tail // 128 * 128

    def update(to):
        def some(cols):
            value = jnp.dot(rounded[0], rec[0, :, cols], preferred_element_type=jnp.float32)
            return value + jnp.dot(rounded[1], rec[1, :, cols], preferred_element_type=jnp.float32)

        @pl.when(to < 7)
        def _():
            upd[to] = some(pl.ds(pl.multiple_of(to * block, 128), block))

        @pl.when(to == 7)
        def _():
            upd[7, :, whole:] = jnp.zeros((FRAMES, block - whole), jnp.float32)
            upd[7, :, :tail] = some(slice(7 * block, actuators))

    def b_dev(zpos):
        return (x, (zpos * 2 + y) * 2 + (core + turn(z) + turn(zpos)) % 2)

    copies = []
    for n in range(7):
        to = block_of(*offsets[n])
        update(to)
        copies.append(remote(upd.at[to], gathered.at[n], a_send.at[n], a_recv.at[n], plane(n)))
    update(me)
    for copy in copies:
        copy.wait_recv()
    drain = copies
    total = upd[me]
    for n in range(7):
        total = total + gathered[n]
    zsum[z] = total
    copies = []
    for k in range(1, depth):
        copies.append(
            remote(zsum.at[z], zsum.at[z], b_send.at[k - 1], b_recv.at[k - 1], b_dev((z + k) % depth))
        )
    for copy in copies:
        copy.wait_recv()
    drain = drain + copies
    total = zsum[0]
    for k in range(1, depth):
        total = total + zsum[k]
    limits = sat[me].astype(jnp.float32) * code_step
    first_cmd = jnp.clip(loop_gain * total[:1], -limits, limits)
    second_cmd = jnp.clip(first_cmd + loop_gain * total[1:], -limits, limits)
    gathered[0, :1] = first_cmd
    gathered[0, 1:] = second_cmd
    own_cols = pl.ds(pl.multiple_of(me * block, 128), block)
    upd_out[:, own_cols] = gathered[0]
    copies = []
    for n in range(7):
        copies.append(
            remote(upd_out.at[:, own_cols], upd_out.at[:, own_cols], c_send.at[n], c_recv.at[n], plane(n))
        )
    for copy in list(x_copies.values()) + list(y_copies.values()) + list(passed.values()):
        copy.wait_send()
    for n, (zpos, slot_at) in enumerate(sends):
        for i in range(count):
            z_copy(n, slot_at, i, zpos).wait_send()

    @pl.when(jnp.logical_not(outer))
    def _():
        for i in range(count):
            z_copy(2, 1, i, z - ahead).wait_send()

    @pl.when(low_end & corner_from)
    def _():
        far_copy.wait_send()

    for copy in copies:
        copy.wait()
    for copy in drain:
        copy.wait_send()


def fused_shards(screens, row_offset, col_offset, layer_bin, illumination, reconstructor, sat_code):
    layer_dev, rows_here, columns = screens.shape
    count_here = illumination.shape[1]
    actuators = reconstructor.shape[2]
    depth = PLANES
    arcs = count_here // LENSLETS
    chunk = (packed_tiles(arcs) * 8, 128)
    edge = ((tile_of(arcs, 1, PUPIL_PIX // 128) + 1) * 8, 128)
    rows = padded_rows(arcs)
    block = -(-actuators // (8 * 128)) * 128
    contraction = FRAMES * 2 * 2 * layer_dev * 4 * rows_here
    width = (FRAMES - 1) * WIDE + PUPIL_PIX
    dma = pltpu.SemaphoreType.DMA
    spots = (FRAMES, GUIDE_STARS, row_offset.shape[1])
    vmem = pl.BlockSpec(memory_space=pltpu.VMEM)

    def in_hbm(value):
        return pltpu.with_memory_space_constraint(value, pltpu.HBM)

    slopes, updates = pl.pallas_call(
        functools.partial(fused_kernel, block),
        out_shape=(
            jax.ShapeDtypeStruct((FRAMES, 2, count_here), jnp.float32),
            jax.ShapeDtypeStruct((FRAMES, 8 * block), jnp.float32),
        ),
        in_specs=[pl.BlockSpec(memory_space=pltpu.HBM)] * 7,
        out_specs=(vmem, vmem),
        scratch_shapes=[
            pltpu.VMEM(screens.shape, jnp.bfloat16),
            pltpu.SMEM(spots, jnp.int32),
            pltpu.SMEM(spots, jnp.int32),
            pltpu.SMEM(layer_bin.shape, jnp.int32),
            pltpu.VMEM(illumination.shape, jnp.float32),
            pltpu.VMEM((2 * layer_dev, 4, rows_here, columns), jnp.float32),
            pltpu.VMEM((2 * layer_dev, columns, width), jnp.bfloat16),
            pltpu.VMEM((depth * rows, contraction), jnp.bfloat16),
            pltpu.VMEM((contraction, PUPIL_PIX), jnp.bfloat16),
            pltpu.VMEM((depth * rows, PUPIL_PIX), jnp.float32),
            pltpu.VMEM((depth,) + chunk, jnp.float32),
            pltpu.VMEM((3,) + chunk, jnp.float32),
            pltpu.VMEM(edge, jnp.float32),
            pltpu.VMEM(chunk, jnp.float32),
            pltpu.VMEM((PIXELS, FRAMES * PIXELS, count_here), jnp.float32),
            pltpu.VMEM((PIXELS, FRAMES * PIXELS, count_here), jnp.float32),
            pltpu.VMEM((2, FRAMES, count_here), jnp.float32),
            pltpu.VMEM(reconstructor.shape, jnp.bfloat16),
            pltpu.VMEM((8, FRAMES, block), jnp.float32),
            pltpu.VMEM((7, FRAMES, block), jnp.float32),
            pltpu.VMEM((depth, FRAMES, block), jnp.float32),
            pltpu.VMEM((actuators,), jnp.int32),
            pltpu.VMEM((8, 1, block), jnp.int32),
            dma((5,)), dma, dma,
            dma((2 * layer_dev * HALVES,)), dma((2 * layer_dev * HALVES,)),
            dma((2 * HALVES,)), dma((2 * HALVES,)),
            dma((2 + 6 * HALVES,)), dma((2 + 6 * HALVES,)),
            dma((6,)), dma((6,)), dma, dma,
            pltpu.SemaphoreType.REGULAR((2,)),
            dma((7,)), dma((7,)),
            dma((depth - 1,)), dma((depth - 1,)),
            dma((7,)), dma((7,)),
        ],
        compiler_params=pltpu.CompilerParams(collective_id=0, has_side_effects=True, vmem_limit_bytes=44 * 2**20),
        name="fused",
    )(
        in_hbm(screens),
        in_hbm(row_offset.transpose(0, 2, 1)),
        in_hbm(col_offset.transpose(0, 2, 1)),
        in_hbm(layer_bin),
        in_hbm(illumination),
        in_hbm(reconstructor),
        in_hbm(sat_code),
    )
    return slopes, updates[:, :actuators]


def step(screens, row_offset, col_offset, layer_bin, illumination, reconstructor, sat_code):
    strips = lax.axis_size("strip")
    fused = (
        lax.axis_size("alt") == 2 == GUIDE_STARS
        and strips == 4 * PLANES
        and screens.shape[0] == 2
        and LENSLETS % strips == 0
        and LENSLETS // strips > 2
        and screens.shape[1] % 16 == 0
        and far_pattern(strips * screens.shape[1], LENSLETS // strips)
    )
    chosen = fused_shards if fused else shards
    return chosen(screens, row_offset, col_offset, layer_bin, illumination, reconstructor, sat_code)


def solution(mesh):
    placed = (
        P("alt", "strip", None),
        P(),
        P(),
        P(),
        P(None, ("alt", "strip")),
        P(None, ("alt", "strip"), None),
        P(),
    )
    return jax.shard_map(
        step,
        mesh=mesh,
        in_specs=placed,
        out_specs=(P(None, None, ("alt", "strip")), P()),
        check_vma=False,
    )
```

```python
import functools
import math

import jax
import jax.numpy as jnp
from jax import lax
from jax.experimental import pallas as pl
from jax.experimental.pallas import tpu as pltpu
from jax.sharding import PartitionSpec as P

LENSLETS = 80
PIXELS = 4
GUIDE_STARS = 2
FRAMES = 2
ACTUATORS = 6000
PUPIL_PIX = 320
WINDOW = 384
SUBAPS_ALL = 12800


highest = lax.Precision.HIGHEST
loop_gain = 0.5
code_step = 0.125
bin_step = 0.03125


def bilinear(offsets):
    return jnp.maximum(0.0, 1.0 - jnp.abs(offsets))


def dft_tables():
    padded = 2 * PIXELS
    freq_index = jnp.arange(padded * padded, dtype=jnp.int32)
    freq_row = freq_index // padded
    freq_col = freq_index % padded
    pix_index = jnp.arange(PIXELS * PIXELS, dtype=jnp.int32)
    pix_row = pix_index // PIXELS
    pix_col = pix_index % PIXELS
    turn_count = (
        freq_row[:, None] * pix_row[None, :] + freq_col[:, None] * pix_col[None, :]
    ) % padded
    angles = turn_count.astype(jnp.float32) * (2.0 * math.pi / padded)
    coord_row = ((freq_row + PIXELS) % padded - PIXELS).astype(jnp.float32)
    coord_col = ((freq_col + PIXELS) % padded - PIXELS).astype(jnp.float32)
    return (jnp.cos(angles), jnp.sin(angles), coord_row, coord_col)


def centroids(pupil_phase, illumination, tables):
    cosine, sine_table, coord_row, coord_col = tables
    field_re = illumination * jnp.cos(pupil_phase)
    field_im = illumination * jnp.sin(pupil_phase)
    real_part = jnp.dot(cosine, field_re, precision=highest) + jnp.dot(
        sine_table, field_im, precision=highest
    )
    imag_part = jnp.dot(cosine, field_im, precision=highest) - jnp.dot(
        sine_table, field_re, precision=highest
    )
    intensity = real_part * real_part + imag_part * imag_part
    flux_sum = jnp.sum(intensity, axis=0)
    slope_row = jnp.sum(intensity * coord_row[:, None], axis=0) / flux_sum
    slope_col = jnp.sum(intensity * coord_col[:, None], axis=0) / flux_sum
    return jnp.stack([slope_row, slope_col])


def shards(screens, row_offset, col_offset, layer_bin, illumination, reconstructor, sat_code):
    layer_dev = screens.shape[0]
    rows_here = screens.shape[1]
    count_here = illumination.shape[1]
    group_pos = lax.axis_index("alt")
    strip_pos = lax.axis_index("strip")
    row_global = strip_pos * rows_here + jnp.arange(rows_here, dtype=jnp.int32)
    pupil_idx = jnp.arange(PUPIL_PIX, dtype=jnp.float32)
    window_idx = jnp.arange(WINDOW, dtype=jnp.float32)
    widened_layers = [
        jnp.pad(screens[layer_no], ((0, 0), (0, WINDOW))) for layer_no in range(layer_dev)
    ]
    frame_terms = []
    for frame_no in range(FRAMES):
        running = jnp.zeros((PIXELS, PIXELS, GUIDE_STARS, LENSLETS, LENSLETS), jnp.float32)
        for layer_no in range(layer_dev):
            layer_pos = group_pos * layer_dev + layer_no
            tops = lax.dynamic_index_in_dim(row_offset[frame_no], layer_pos, 0, keepdims=False)
            lefts = lax.dynamic_index_in_dim(col_offset[frame_no], layer_pos, 0, keepdims=False)
            bin_value = lax.dynamic_index_in_dim(layer_bin, layer_pos, 0, keepdims=False)
            shrink = 1.0 - bin_value.astype(jnp.float32) * bin_step
            col_weights = bilinear(window_idx[None, :] - pupil_idx[:, None] * shrink)
            widened = widened_layers[layer_no]

            def cut_columns(left_col):
                return lax.dynamic_slice_in_dim(widened, left_col, WINDOW, 1)

            strips = jax.vmap(cut_columns)(lefts).astype(jnp.float32)
            across = jnp.einsum("drc,jc->drj", strips, col_weights, precision=highest)
            offsets = (row_global[None, :] - tops[:, None]).astype(jnp.float32)
            row_weights = bilinear(offsets[:, None, :] - pupil_idx[None, :, None] * shrink)
            running = running + jnp.einsum(
                "dapr,drbq->pqdab",
                row_weights.reshape(GUIDE_STARS, LENSLETS, PIXELS, rows_here),
                across.reshape(GUIDE_STARS, rows_here, LENSLETS, PIXELS),
                precision=highest,
            )
        frame_terms.append(running.reshape(PIXELS * PIXELS, SUBAPS_ALL))
    phase_terms = jnp.concatenate(frame_terms, axis=0)
    partly = lax.psum_scatter(phase_terms, "alt", scatter_dimension=1, tiled=True)
    owned = lax.psum_scatter(partly, "strip", scatter_dimension=1, tiled=True)
    pupil_phase = owned.reshape(FRAMES, PIXELS * PIXELS, count_here)
    tables = dft_tables()
    slopes = jnp.stack(
        [centroids(pupil_phase[frame_no], illumination, tables) for frame_no in range(FRAMES)]
    )
    rounded = slopes.astype(jnp.bfloat16).reshape(FRAMES, 2 * count_here)
    partial_value = jnp.dot(
        rounded,
        reconstructor.reshape(2 * count_here, ACTUATORS),
        preferred_element_type=jnp.float32,
    )
    updates = lax.psum(partial_value, ("alt", "strip"))
    limits = sat_code.astype(jnp.float32) * code_step
    first_cmd = jnp.clip(loop_gain * updates[0], -limits, limits)
    second_cmd = jnp.clip(first_cmd + loop_gain * updates[1], -limits, limits)
    return (slopes, jnp.stack([first_cmd, second_cmd]))


MESH = pl.DeviceIdType.MESH
HALVES = 1
PLANES = 4
WIDE = -(-PUPIL_PIX // 128) * 128


def pair_gain(distance):
    turn = 2.0 * math.pi / (2 * PIXELS)
    return 4.0 * sum(k * math.sin(turn * k * distance) for k in range(1, PIXELS))


def padded_rows(arcs):
    return -(-arcs * FRAMES * PIXELS // 16) * 16


def tile_of(arcs, arc, part):
    full = PUPIL_PIX // 128
    pair = arc // 2 * (2 * full + 1)
    if part < full:
        return pair + arc % 2 * full + part
    return pair + (2 * full if arc // 2 * 2 + 1 < arcs else full)


def packed_tiles(arcs):
    return tile_of(arcs, arcs - 1, PUPIL_PIX // 128) + 1


def reaches(total, rows, first, last):
    for layer_bin in range(16):
        shrink = 1.0 - layer_bin * bin_step
        top = math.floor(total - 1 - (PUPIL_PIX - 1) * shrink)
        if top + last * shrink > rows[0] - 1 and first * shrink < rows[1] + 1:
            return True
    return False


def far_pattern(total, arcs):
    plane_rows = total // PLANES
    strip_rows = arcs * PIXELS
    for strip in range(4):
        first = strip * strip_rows
        if reaches(total, (total - plane_rows, total - 1), first, first + strip_rows - 1):
            return False
        first += (PLANES - 1) * 4 * strip_rows
        low = first + 2 * PIXELS if strip == 0 else first
        if reaches(total, (0, plane_rows - 1), low, first + strip_rows - 1):
            return False
    return True


def fused_kernel(
    block,
    scr_hbm,
    row_hbm,
    col_hbm,
    bin_hbm,
    ill_hbm,
    rec_hbm,
    sat_hbm,
    slopes_out,
    upd_out,
    scr_ref,
    row_ref,
    col_ref,
    bin_ref,
    ill_ref,
    scr_all,
    colw,
    roww,
    rhs,
    acc,
    part,
    z_in,
    far_in,
    phase_sc,
    phiq,
    illq,
    slope_sc,
    rec,
    upd,
    gathered,
    zsum,
    sat_raw,
    sat,
    in_sem,
    rec_sem,
    sat_sem,
    own_send,
    own_recv,
    pass_send,
    pass_recv,
    core_send,
    core_recv,
    z_send,
    z_recv,
    far_send,
    far_recv,
    credit,
    a_send,
    a_recv,
    b_send,
    b_recv,
    c_send,
    c_recv,
):
    layer_dev, rows_here, columns = scr_ref.shape
    count_here = ill_ref.shape[1]
    arcs = count_here // LENSLETS
    chunk_rows = padded_rows(arcs)
    depth = PLANES
    full = PUPIL_PIX // 128
    rest = PUPIL_PIX - full * 128
    actuators = rec_hbm.shape[2]

    loads = [
        pltpu.make_async_copy(src, dst, in_sem.at[n])
        for n, (src, dst) in enumerate(
            (
                (scr_hbm, scr_ref),
                (row_hbm, row_ref),
                (col_hbm, col_ref),
                (bin_hbm, bin_ref),
                (ill_hbm, ill_ref),
            )
        )
    ]
    for load in loads:
        load.start()
    rec_copy = pltpu.make_async_copy(rec_hbm, rec, rec_sem)
    rec_copy.start()
    sat_load = pltpu.make_async_copy(sat_hbm, sat_raw, sat_sem)
    sat_load.start()

    x = lax.axis_index("alt")
    strip = lax.axis_index("strip")
    core = strip % 2
    y = (strip // 2) % 2
    z = strip // 4

    offsets = ((1, 1, 0), (1, 1, 1), (1, 0, 0), (0, 1, 0), (1, 0, 1), (0, 1, 1), (0, 0, 1))

    def plane(n):
        dx, dy, dc = offsets[n]
        return ((x + dx) % 2, (z * 2 + (y + dy) % 2) * 2 + (core + dc) % 2)

    def block_of(dx, dy, dc):
        return ((x + dx) % 2 * 2 + (y + dy) % 2) * 2 + (core + dc + turn(z)) % 2

    def turn(zpos):
        return (zpos >= depth // 2).astype(jnp.int32)

    me = block_of(0, 0, 0)

    def depth_dev(zpos):
        return (x, (zpos * 2 + y) * 2 + core)

    def depth_swap(zpos):
        return (x, (zpos * 2 + y) * 2 + 1 - core)

    x_dev = (1 - x, (z * 2 + y) * 2 + 1 - core)
    y_dev = (x, (z * 2 + 1 - y) * 2 + 1 - core)
    core_dev = (x, (z * 2 + y) * 2 + 1 - core)
    low_end = z == 0
    high_end = z == depth - 1
    outer = low_end | high_end
    corner_from = (y == 0) & (core == 1)
    corner_to = (y == 0) & (core == 0)

    barrier = pltpu.get_barrier_semaphore()
    for device in (x_dev, y_dev, core_dev):
        pl.semaphore_signal(barrier, inc=1, device_id=device, device_id_type=MESH)

    @pl.when(jnp.logical_not(low_end))
    def _():
        pl.semaphore_signal(barrier, inc=1, device_id=depth_swap(z - 1), device_id_type=MESH)

    @pl.when(jnp.logical_not(high_end))
    def _():
        pl.semaphore_signal(barrier, inc=1, device_id=depth_swap(z + 1), device_id_type=MESH)

    spot = y * 2 + core
    other = (1 - y) * 2 + core
    spot_in = y * 2 + 1 - core
    other_in = (1 - y) * 2 + 1 - core
    loads[0].wait()
    for li in range(layer_dev):
        scr_all[x * layer_dev + li, spot] = scr_ref[li].astype(jnp.float32)

    @pl.when(outer)
    def _():
        pl.semaphore_wait(barrier, 4)

    @pl.when(jnp.logical_not(outer))
    def _():
        pl.semaphore_wait(barrier, 5)

    def remote(src, dst, send, recv, device):
        copy = pltpu.make_async_remote_copy(
            src_ref=src, dst_ref=dst, send_sem=send, recv_sem=recv, device_id=device, device_id_type=MESH
        )
        copy.start()
        return copy

    half = rows_here // HALVES

    def piece(layer, at, h):
        return scr_all.at[layer, at, pl.ds(h * half, half)]

    def share(which, li, h, device):
        n = (which * layer_dev + li) * HALVES + h
        here = piece(x * layer_dev + li, spot, h)
        return remote(here, here, own_send.at[n], own_recv.at[n], device)

    x_copies, y_copies = {}, {}
    for step in range(layer_dev):
        for h in range(HALVES):
            x_copies[step, h] = share(0, step, h, x_dev)
            y_copies[layer_dev - 1 - step, h] = share(1, layer_dev - 1 - step, h, y_dev)
    core_copies = []

    def to_core(here):
        n = len(core_copies)
        core_copies.append(remote(here, here, core_send.at[n], core_recv.at[n], core_dev))

    to_core(scr_all.at[x * layer_dev, spot])
    to_core(scr_all.at[x * layer_dev + 1, spot])

    for load in loads[1:]:
        load.wait()

    layers = [((x + rel) % 2) * layer_dev + li for rel in range(2) for li in range(layer_dev)]
    shrinks = [1.0 - bin_ref[layer].astype(jnp.float32) * bin_step for layer in layers]
    tops = [[row_ref[f, x, layer].astype(jnp.float32) for layer in layers] for f in range(FRAMES)]
    lefts = [[col_ref[f, x, layer].astype(jnp.float32) for layer in layers] for f in range(FRAMES)]

    width = colw.shape[2]
    col_pos = lax.broadcasted_iota(jnp.int32, (columns, width), 0).astype(jnp.float32)
    lane = lax.broadcasted_iota(jnp.int32, (1, width), 1)
    second = lane >= WIDE
    lane = jnp.where(second, lane - WIDE, lane)
    q_of = (
        (lane >= LENSLETS).astype(jnp.int32)
        + (lane >= 2 * LENSLETS).astype(jnp.int32)
        + (lane >= 3 * LENSLETS).astype(jnp.int32)
    )
    pupil_col = ((lane - q_of * LENSLETS) * PIXELS + q_of).astype(jnp.float32)

    def column_weights(n):
        start = pupil_col * shrinks[n] + jnp.where(second, lefts[1][n], lefts[0][n])
        colw[n] = bilinear(col_pos - start).astype(jnp.bfloat16)

    mine = range(layer_dev)
    theirs = range(layer_dev, 2 * layer_dev)
    pair = 2 * rows_here
    stages = (
        (mine, 2 * y, pair),
        (theirs, 2 * y, pair),
        (mine, 2 * (1 - y), pair),
        (theirs, other, rows_here),
        (theirs, 2 * (1 - y) + 1 - core, rows_here),
    )
    begins = [0]
    for members, at, rows in stages:
        begins.append(begins[-1] + len(members) * FRAMES * 2 * rows)

    def row_weights(number):
        members, at, rows = stages[number]
        seg = 2 * rows
        row_pos = lax.broadcasted_iota(jnp.int32, (chunk_rows, seg), 1) % rows + (z * 4 + at) * rows_here
        row_pos = row_pos.astype(jnp.float32)
        row_sub = lax.broadcasted_iota(jnp.int32, (chunk_rows, seg), 0)
        row_base = row_sub // 8 * PIXELS + row_sub % PIXELS
        row_frame = row_sub // PIXELS % FRAMES
        for zpos in range(depth):
            held = jnp.where(z == zpos, core, 1 - core)
            pupil_row = (row_base + ((zpos * 2 + y) * 2 + held) * (arcs * PIXELS)).astype(jnp.float32)
            for i, n in enumerate(members):
                reach = pupil_row * shrinks[n]
                for f in range(FRAMES):
                    weight = jnp.where(row_frame == f, bilinear(row_pos - tops[f][n] - reach), 0.0)
                    lo = begins[number] + (i * FRAMES + f) * seg
                    roww[zpos * chunk_rows : (zpos + 1) * chunk_rows, lo : lo + seg] = weight.astype(jnp.bfloat16)

    def across(number, n):
        members, at, rows = stages[number]
        blocks = rows // rows_here
        source = scr_all[layers[n], pl.ds(at, blocks)].reshape(rows, columns).astype(jnp.bfloat16)
        value = jnp.dot(source, colw[n], preferred_element_type=jnp.float32)
        for f in range(FRAMES):
            one = value[:, f * WIDE : f * WIDE + PUPIL_PIX]
            high = one.astype(jnp.bfloat16)
            low = (one - high.astype(jnp.float32)).astype(jnp.bfloat16)
            lo = begins[number] + ((n - members[0]) * FRAMES + f) * 2 * rows
            rhs[lo : lo + rows, :] = high
            rhs[lo + rows : lo + 2 * rows, :] = low

    def project(number):
        lo, hi = begins[number], begins[number + 1]
        return jnp.dot(roww[:, lo:hi], rhs[lo:hi, :], preferred_element_type=jnp.float32)

    for n in range(2 * layer_dev):
        column_weights(n)
    for number in range(len(stages)):
        row_weights(number)

    passed = {}

    def pass_on(which, h, here, device):
        n = which * HALVES + h
        passed[which, h] = remote(here, here, pass_send.at[n], pass_recv.at[n], device)

    for h in range(HALVES):
        here = piece((1 - x) * layer_dev, spot_in, h)
        x_copies[0, h].wait_recv()
        pass_on(0, h, here, y_dev)
        to_core(here)
        here = piece(x * layer_dev + 1, other_in, h)
        y_copies[1, h].wait_recv()
        pass_on(1, h, here, x_dev)
        to_core(here)
    for copy in core_copies[:2]:
        copy.wait()

    @pl.when(jnp.logical_not(outer))
    def _():
        for zpos in (z - 1, z + 1):
            pl.semaphore_signal(credit.at[0], inc=1, device_id=depth_dev(zpos), device_id_type=MESH)

    for n in mine:
        across(0, n)
    acc[...] = project(0)
    for p in range(PIXELS):
        for q in range(PIXELS):
            for f in range(FRAMES):
                illq[q, f * PIXELS + p : f * PIXELS + p + 1, :] = ill_ref[p * PIXELS + q : p * PIXELS + q + 1, :]
    sat_load.wait()
    for n in range(8):
        some = min(block, actuators - n * block)
        sat[n, 0, :some] = sat_raw[n * block : n * block + some]
    pl.semaphore_wait(credit.at[0], 1)

    @pl.when((z == 1) & corner_from)
    def _():
        pl.semaphore_signal(credit.at[1], inc=1, device_id=depth_dev(z - 1), device_id_type=MESH)

    for h in range(HALVES):
        x_copies[1, h].wait_recv()
        to_core(piece((1 - x) * layer_dev + 1, spot_in, h))
        y_copies[0, h].wait_recv()
        to_core(piece(x * layer_dev, other_in, h))
    for copy in core_copies[2 : 2 + 2 * HALVES]:
        copy.wait()
    across(1, layer_dev)
    across(2, 1)
    for copy in core_copies[2 + 2 * HALVES : 2 + 4 * HALVES]:
        copy.wait()
    across(1, layer_dev + 1)
    across(2, 0)
    for h in range(HALVES):
        passed[0, h].wait_recv()
        to_core(piece((1 - x) * layer_dev, other, h))
        passed[1, h].wait_recv()
        to_core(piece((1 - x) * layer_dev + 1, other, h))
    acc[...] += project(1) + project(2)
    for n in theirs:
        across(3, n)
    acc[...] += project(3)
    for copy in core_copies[2 + 4 * HALVES :]:
        copy.wait()
    for n in theirs:
        across(4, n)
    acc[...] += project(4)
    def pack(zpos):
        value = acc[pl.ds(pl.multiple_of(zpos * chunk_rows, chunk_rows), chunk_rows), :]
        for a in range(arcs):
            lines = value[a * 8 : (a + 1) * 8]
            for t in range(full):
                at = tile_of(arcs, a, t) * 8
                part[zpos, at : at + 8, :] = lines[:, t * 128 : (t + 1) * 128]
            at = tile_of(arcs, a, full) * 8
            lane0 = a % 2 * rest
            part[zpos, at : at + 8, lane0 : lane0 + rest] = lines[:, full * 128 :]
        if arcs % 2:
            at = tile_of(arcs, arcs - 1, full) * 8
            part[zpos, at : at + 8, rest:] = jnp.zeros((8, 128 - rest), jnp.float32)

    edge = tile_of(arcs, 1, full) + 1
    tiles = packed_tiles(arcs)
    pieces = [pl.ds(edge * 8, (tiles - edge) * 8), pl.ds(0, edge * 8)]
    count = len(pieces)
    ahead = jnp.where(z < depth // 2, 1, -1)

    def z_copy(send, slot_at, i, zpos):
        return pltpu.make_async_remote_copy(
            src_ref=part.at[zpos, pieces[i]],
            dst_ref=z_in.at[slot_at, pieces[i]],
            send_sem=z_send.at[send * count + i],
            recv_sem=z_recv.at[slot_at * count + i],
            device_id=depth_swap(zpos),
            device_id_type=MESH,
        )

    far_copy = pltpu.make_async_remote_copy(
        src_ref=part.at[depth - 1, pieces[1]],
        dst_ref=far_in,
        send_sem=far_send,
        recv_sem=far_recv,
        device_id=depth_swap(depth - 1),
        device_id_type=MESH,
    )
    sends = [(z + 2 * ahead, 0), (z + ahead, jnp.where(outer, 2, 1))]
    @pl.when(jnp.logical_not(outer))
    def _():
        pack(z - ahead)
        for i in range(count):
            z_copy(2, 1, i, z - ahead).start()

    pack(sends[0][0])
    for i in range(count):
        z_copy(0, sends[0][1], i, sends[0][0]).start()

    pack(sends[1][0])
    for i in range(count):
        z_copy(1, sends[1][1], i, sends[1][0]).start()

    @pl.when(low_end & corner_from)
    def _():
        pack(depth - 1)
        pl.semaphore_wait(credit.at[1], 1)
        far_copy.start()

    pack(z)
    for i, rows in enumerate(pieces):

        @pl.when(jnp.logical_not(outer))
        def _():
            z_copy(0, 2, i, z - ahead).wait_recv()
            part[z, rows] = part[z, rows] + z_in[2, rows]

        z_copy(0, 1, i, z + ahead).wait_recv()
        z_copy(0, 0, i, z + 2 * ahead).wait_recv()
        phase_sc[rows] = part[z, rows] + z_in[0, rows] + z_in[1, rows]

    @pl.when(high_end & corner_to)
    def _():
        far_copy.wait_recv()
        phase_sc[pieces[1]] = phase_sc[pieces[1]] + far_in[...]

    for a in range(arcs):
        for q in range(PIXELS):
            lo = q * LENSLETS
            while lo < (q + 1) * LENSLETS:
                t = lo // 128
                hi = min((q + 1) * LENSLETS, (t + 1) * 128)
                at = tile_of(arcs, a, t) * 8
                lane0 = lo - t * 128 + (a % 2 * rest if t == full else 0)
                to = a * LENSLETS + lo - q * LENSLETS
                phiq[q, :, to : to + hi - lo] = phase_sc[at : at + 8, lane0 : lane0 + hi - lo]
                lo = hi

    cosines, sines = [], []
    flux = None
    for q in range(PIXELS):
        amp = illq[q]
        phi = phiq[q]
        cosines.append(amp * jnp.cos(phi))
        sines.append(amp * jnp.sin(phi))
        flux = amp * amp if flux is None else flux + amp * amp
    tip = -float(PIXELS) * flux
    tilt = tip
    pix_row = lax.broadcasted_iota(jnp.int32, flux.shape, 0) % PIXELS
    for d in range(1, PIXELS):
        gain = pair_gain(d)
        even = -2.0 * PIXELS * (-1.0) ** d
        term = None
        for q in range(d, PIXELS):
            ch, sh, cl, sl = cosines[q], sines[q], cosines[q - d], sines[q - d]
            new = gain * (sh * cl - ch * sl) + even * (ch * cl + sh * sl)
            term = new if term is None else term + new
        tilt = tilt + term
        term = None
        for q in range(PIXELS):
            ch, sh = cosines[q], sines[q]
            cl, sl = pltpu.roll(ch, d, 0), pltpu.roll(sh, d, 0)
            new = gain * (sh * cl - ch * sl) + even * (ch * cl + sh * sl)
            term = new if term is None else term + new
        tip = tip + jnp.where(pix_row >= d, term, 0.0)
    for f in range(FRAMES):
        rows = slice(f * PIXELS, (f + 1) * PIXELS)
        total = jnp.sum(flux[rows], axis=0, keepdims=True) * (2.0 * PIXELS)
        for c, value in enumerate((tip, tilt)):
            slope = jnp.sum(value[rows], axis=0, keepdims=True) / total
            slopes_out[f, c : c + 1, :] = slope
            slope_sc[c, f : f + 1, :] = slope

    rec_copy.wait()
    rounded = [slope_sc[c].astype(jnp.bfloat16) for c in range(2)]
    tail = actuators - 7 * block
    whole = tail // 128 * 128

    def update(to):
        def some(cols):
            value = jnp.dot(rounded[0], rec[0, :, cols], preferred_element_type=jnp.float32)
            return value + jnp.dot(rounded[1], rec[1, :, cols], preferred_element_type=jnp.float32)

        @pl.when(to < 7)
        def _():
            upd[to] = some(pl.ds(pl.multiple_of(to * block, 128), block))

        @pl.when(to == 7)
        def _():
            upd[7, :, whole:] = jnp.zeros((FRAMES, block - whole), jnp.float32)
            upd[7, :, :tail] = some(slice(7 * block, actuators))

    def b_dev(zpos):
        return (x, (zpos * 2 + y) * 2 + (core + turn(z) + turn(zpos)) % 2)

    copies = []
    for n in range(7):
        to = block_of(*offsets[n])
        update(to)
        copies.append(remote(upd.at[to], gathered.at[n], a_send.at[n], a_recv.at[n], plane(n)))
    update(me)
    for copy in copies:
        copy.wait_recv()
    drain = copies
    total = upd[me]
    for n in range(7):
        total = total + gathered[n]
    zsum[z] = total
    copies = []
    for k in range(1, depth):
        copies.append(
            remote(zsum.at[z], zsum.at[z], b_send.at[k - 1], b_recv.at[k - 1], b_dev((z + k) % depth))
        )
    for copy in copies:
        copy.wait_recv()
    drain = drain + copies
    total = zsum[0]
    for k in range(1, depth):
        total = total + zsum[k]
    limits = sat[me].astype(jnp.float32) * code_step
    first_cmd = jnp.clip(loop_gain * total[:1], -limits, limits)
    second_cmd = jnp.clip(first_cmd + loop_gain * total[1:], -limits, limits)
    gathered[0, :1] = first_cmd
    gathered[0, 1:] = second_cmd
    own_cols = pl.ds(pl.multiple_of(me * block, 128), block)
    upd_out[:, own_cols] = gathered[0]
    copies = []
    for n in range(7):
        copies.append(
            remote(upd_out.at[:, own_cols], upd_out.at[:, own_cols], c_send.at[n], c_recv.at[n], plane(n))
        )
    for copy in list(x_copies.values()) + list(y_copies.values()) + list(passed.values()):
        copy.wait_send()
    for n, (zpos, slot_at) in enumerate(sends):
        for i in range(count):
            z_copy(n, slot_at, i, zpos).wait_send()

    @pl.when(jnp.logical_not(outer))
    def _():
        for i in range(count):
            z_copy(2, 1, i, z - ahead).wait_send()

    @pl.when(low_end & corner_from)
    def _():
        far_copy.wait_send()

    for copy in copies:
        copy.wait()
    for copy in drain:
        copy.wait_send()


def fused_shards(screens, row_offset, col_offset, layer_bin, illumination, reconstructor, sat_code):
    layer_dev, rows_here, columns = screens.shape
    count_here = illumination.shape[1]
    actuators = reconstructor.shape[2]
    depth = PLANES
    arcs = count_here // LENSLETS
    chunk = (packed_tiles(arcs) * 8, 128)
    edge = ((tile_of(arcs, 1, PUPIL_PIX // 128) + 1) * 8, 128)
    rows = padded_rows(arcs)
    block = -(-actuators // (8 * 128)) * 128
    contraction = FRAMES * 2 * 2 * layer_dev * 4 * rows_here
    width = (FRAMES - 1) * WIDE + PUPIL_PIX
    dma = pltpu.SemaphoreType.DMA
    spots = (FRAMES, GUIDE_STARS, row_offset.shape[1])
    vmem = pl.BlockSpec(memory_space=pltpu.VMEM)

    def in_hbm(value):
        return pltpu.with_memory_space_constraint(value, pltpu.HBM)

    slopes, updates = pl.pallas_call(
        functools.partial(fused_kernel, block),
        out_shape=(
            jax.ShapeDtypeStruct((FRAMES, 2, count_here), jnp.float32),
            jax.ShapeDtypeStruct((FRAMES, 8 * block), jnp.float32),
        ),
        in_specs=[pl.BlockSpec(memory_space=pltpu.HBM)] * 7,
        out_specs=(vmem, vmem),
        scratch_shapes=[
            pltpu.VMEM(screens.shape, jnp.bfloat16),
            pltpu.SMEM(spots, jnp.int32),
            pltpu.SMEM(spots, jnp.int32),
            pltpu.SMEM(layer_bin.shape, jnp.int32),
            pltpu.VMEM(illumination.shape, jnp.float32),
            pltpu.VMEM((2 * layer_dev, 4, rows_here, columns), jnp.float32),
            pltpu.VMEM((2 * layer_dev, columns, width), jnp.bfloat16),
            pltpu.VMEM((depth * rows, contraction), jnp.bfloat16),
            pltpu.VMEM((contraction, PUPIL_PIX), jnp.bfloat16),
            pltpu.VMEM((depth * rows, PUPIL_PIX), jnp.float32),
            pltpu.VMEM((depth,) + chunk, jnp.float32),
            pltpu.VMEM((3,) + chunk, jnp.float32),
            pltpu.VMEM(edge, jnp.float32),
            pltpu.VMEM(chunk, jnp.float32),
            pltpu.VMEM((PIXELS, FRAMES * PIXELS, count_here), jnp.float32),
            pltpu.VMEM((PIXELS, FRAMES * PIXELS, count_here), jnp.float32),
            pltpu.VMEM((2, FRAMES, count_here), jnp.float32),
            pltpu.VMEM(reconstructor.shape, jnp.bfloat16),
            pltpu.VMEM((8, FRAMES, block), jnp.float32),
            pltpu.VMEM((7, FRAMES, block), jnp.float32),
            pltpu.VMEM((depth, FRAMES, block), jnp.float32),
            pltpu.VMEM((actuators,), jnp.int32),
            pltpu.VMEM((8, 1, block), jnp.int32),
            dma((5,)), dma, dma,
            dma((2 * layer_dev * HALVES,)), dma((2 * layer_dev * HALVES,)),
            dma((2 * HALVES,)), dma((2 * HALVES,)),
            dma((2 + 6 * HALVES,)), dma((2 + 6 * HALVES,)),
            dma((6,)), dma((6,)), dma, dma,
            pltpu.SemaphoreType.REGULAR((2,)),
            dma((7,)), dma((7,)),
            dma((depth - 1,)), dma((depth - 1,)),
            dma((7,)), dma((7,)),
        ],
        compiler_params=pltpu.CompilerParams(collective_id=0, has_side_effects=True, vmem_limit_bytes=44 * 2**20),
        name="fused",
    )(
        in_hbm(screens),
        in_hbm(row_offset.transpose(0, 2, 1)),
        in_hbm(col_offset.transpose(0, 2, 1)),
        in_hbm(layer_bin),
        in_hbm(illumination),
        in_hbm(reconstructor),
        in_hbm(sat_code),
    )
    return slopes, updates[:, :actuators]


def step(screens, row_offset, col_offset, layer_bin, illumination, reconstructor, sat_code):
    strips = lax.axis_size("strip")
    fused = (
        lax.axis_size("alt") == 2 == GUIDE_STARS
        and strips == 4 * PLANES
        and screens.shape[0] == 2
        and LENSLETS % strips == 0
        and LENSLETS // strips > 2
        and screens.shape[1] % 16 == 0
        and far_pattern(strips * screens.shape[1], LENSLETS // strips)
    )
    chosen = fused_shards if fused else shards
    return chosen(screens, row_offset, col_offset, layer_bin, illumination, reconstructor, sat_code)


def solution(mesh):
    placed = (
        P("alt", "strip", None),
        P(),
        P(),
        P(),
        P(None, ("alt", "strip")),
        P(None, ("alt", "strip"), None),
        P(),
    )
    return jax.shard_map(
        step,
        mesh=mesh,
        in_specs=placed,
        out_specs=(P(None, None, ("alt", "strip")), P()),
        check_vma=False,
    )
```
